32 devices in a mesh: seq: 8 (over y, x, core), grp: 4 (over z).
Axes of the slice: x: 2, y: 2, z: 4, core: 2. Of those that a mesh axis runs over, the one named last changes fastest.
Arguments:
- queries: bfloat16 [8192, 4096], P(('grp', 'seq')), parts along dimension 0, may hold values from -64 to 64
- keys: bfloat16 [8192, 1024], P(('grp', 'seq')), parts along dimension 0, may hold values from -64 to 64
- values: bfloat16 [8192, 1024], P(('grp', 'seq')), parts along dimension 0, may hold values from -6 to 6
- doc_lengths: int32 [24], P('grp'), parts along dimension 0, may hold values from 1 to 8, 16 in all
Outputs:
- attended: bfloat16 [8192, 4096], P(('grp', 'seq')), parts along dimension 0
The draws below stay inside these ranges and needn't reach their ends.
There are 4 independent parts, one for each index of `grp`. The reference program is written for one: setup_inputs(seed, part) draws one part's arguments, and reference() takes and returns one part's arrays. A program takes and returns all parts, laid end to end along the dimension named above; each array names one. Nothing has to cross between parts.
Inputs may be any that keep to these rules, and one draw needn't show every extreme that they name: `doc_lengths`: lengths of the documents in units of 128 tokens, summing to 16.
All inputs are finite; a program needn't handle non-finite values.
Results may differ from the reference program's by a relative error of at most 0.004.
Values may be sent and summed in bfloat16 or wider, within the bound.
No kernel may reach another device: no remote copies, remote signals or barrier semaphores. Data moves between devices by JAX's collectives and lax.ppermute only.
A program may use at most 128 MiB of HBM per device.

```python
import math
import jax
import jax.numpy as jnp
import numpy as np
from jax import lax

HEADS = 32
KV_HEADS = 8
HEAD_DIM = 128
DOC_UNIT = 128
DOCS = 6
TOKENS = 2048
UNITS = 16


def drawn(key):
    base = jax.random.fold_in(key, 7)
    key_a, key_b = jax.random.split(base, 2)
    group_size = HEADS // KV_HEADS
    key_vectors = jax.random.normal(key_a, (TOKENS, KV_HEADS, HEAD_DIM), jnp.float32)
    query_vectors = jax.random.normal(key_b, (TOKENS, KV_HEADS, group_size, HEAD_DIM), jnp.float32)
    return (query_vectors.reshape(TOKENS, HEADS * HEAD_DIM), key_vectors.reshape(TOKENS, KV_HEADS * HEAD_DIM))


def draw_queries(key, part):
    return drawn(key)[0].astype(jnp.bfloat16)


def draw_keys(key, part):
    return drawn(key)[1].astype(jnp.bfloat16)


def shard_levels(own_key, extent, cuts, least, top_value):
    factor_of, own = 1.0, jax.random.fold_in(own_key, 6)
    for dim, shards_of in cuts:
        heights = jnp.exp(jax.random.uniform(jax.random.fold_in(own, dim), (shards_of,), jnp.float32, least / len(cuts), top_value / len(cuts)))
        factor_of = factor_of * jnp.repeat(heights, extent[dim] // shards_of).reshape([-1 if axis == dim else 1 for axis in range(len(extent))])
    return factor_of


def split_up(count, total, reach, skew):
    weights = [(1 << 20) // math.isqrt(grade ** skew) + 1 for grade in range(2, count + 1)]
    surplus, given = total - reach - (count - 1), [1] * (count - 1)
    while surplus > 0:
        free = [i for i in range(count - 1) if given[i] < reach]
        mass, left = sum([weights[i] for i in free]), surplus
        for i in free:
            more = min(reach - given[i], max(1, left * weights[i] // mass), surplus)
            given[i] = given[i] + more
            surplus = surplus - more
    return np.array([reach] + given)


def uneven(rng, amount, total, most, lean):
    if amount == 2:
        one = jax.random.randint(rng, (), max(1, total - most), min(most, total - 1) + 1)
        return jnp.stack([one, total - one])
    tallies = jnp.asarray(split_up(amount, total, most, lean), jnp.int32)
    pairs = (amount - 1) // 2
    giver, sink = tallies[1:1 + 2 * pairs:2], tallies[2:2 + 2 * pairs:2]
    slack = jnp.minimum(giver - 1, most - sink)
    passed = jax.random.randint(jax.random.fold_in(rng, 1), (pairs,), 0, 1 << 20) % (slack + 1)
    tallies = tallies.at[1:1 + 2 * pairs:2].set(giver - passed).at[2:2 + 2 * pairs:2].set(sink + passed)
    return tallies[jax.random.permutation(jax.random.fold_in(rng, 2), amount)]


def centred(stream_key, dims, width, reach, cuts=(), held_as=jnp.bfloat16):
    values = width * jax.random.normal(stream_key, dims, jnp.float32)
    if cuts:
        values = values * shard_levels(stream_key, dims, cuts, -0.22, 0.18)
    return jnp.clip(values, -reach, reach).astype(held_as)


def setup_inputs(seed: int = 0, part: int = 0) -> dict:
    key_list = jax.random.split(jax.random.key(seed), 5)
    own_keys = jax.random.split(jax.random.fold_in(key_list[4], part), 5)
    return {
        "queries": draw_queries(jax.random.fold_in(jax.random.fold_in(key_list[4], part), 71), part),
        "keys": draw_keys(jax.random.fold_in(jax.random.fold_in(key_list[4], part), 71), part),
        "values": centred(own_keys[2], (TOKENS, KV_HEADS * HEAD_DIM), 1.0, 6.0, ((0, 8),)),
        "doc_lengths": uneven(own_keys[3], DOCS, UNITS, UNITS // 2, 2).astype(jnp.int32),
    }


def reference(queries, keys, values, doc_lengths):
    group_size = HEADS // KV_HEADS
    scale = HEAD_DIM ** -0.5
    grouped = queries.reshape(TOKENS, KV_HEADS, group_size, HEAD_DIM).transpose(1, 0, 2, 3)
    key_heads = keys.reshape(TOKENS, KV_HEADS, HEAD_DIM).transpose(1, 0, 2)
    value_heads = values.reshape(TOKENS, KV_HEADS, HEAD_DIM).transpose(1, 0, 2)
    positions = jnp.arange(TOKENS, dtype=jnp.int32)
    lengths = (doc_lengths * DOC_UNIT).astype(jnp.int32)
    starts = (jnp.cumsum(lengths) - lengths).astype(jnp.int32)
    documents = jnp.sum((positions[:, None] >= starts[None, :]).astype(jnp.int32), axis=1)
    block_rows = math.gcd(TOKENS, 1024)
    pieces = []
    for first_row in range(0, TOKENS, block_rows):
        last_row = first_row + block_rows
        allowed = (positions[None, :last_row] <= positions[first_row:last_row, None]) & (
            documents[None, :last_row] == documents[first_row:last_row, None])

        def per_head(operands, allowed=allowed):
            query_head, key_head, value_head = operands
            scores = jnp.einsum("qgd,kd->gqk", query_head.astype(jnp.float32), key_head.astype(jnp.float32)) * scale
            scores = jnp.where(allowed[None], scores, -jnp.inf)
            weights = jnp.exp(scores - jnp.max(scores, axis=-1, keepdims=True))
            totals = jnp.sum(weights, axis=-1)
            rounded = lax.optimization_barrier(weights.astype(jnp.bfloat16)).astype(jnp.float32)
            mixed = jnp.einsum("gqk,kd->qgd", rounded, value_head.astype(jnp.float32))
            return mixed / jnp.transpose(totals)[:, :, None]

        outputs = lax.map(per_head, (grouped[:, first_row:last_row], key_heads[:, :last_row], value_heads[:, :last_row]))
        pieces.append(outputs.transpose(1, 0, 2, 3).reshape(block_rows, HEADS * HEAD_DIM))
    return jnp.concatenate(pieces, axis=0).astype(jnp.bfloat16)
```

```python
import functools
import math

import jax
import jax.numpy as jnp
import numpy as np
from jax import lax
from jax.experimental import pallas as pl
from jax.experimental.pallas import tpu as pltpu
from jax.sharding import PartitionSpec as P

HEAD_DIM = 128
DOC_UNIT = 128
MOST_UNITS = 8
PARTS_OF_HEADS = 2


class Piece:
    def __init__(self, array, units):
        self.array, self.units = array, units

    def rows(self, first, last):
        return Piece(self.array[first * DOC_UNIT : last * DOC_UNIT], self.units[:, first:last])

    def to(self, pairs):
        units = np.full_like(self.units, -1)
        for source, target in pairs:
            units[target] = self.units[source]
        return Piece(lax.ppermute(self.array, "seq", pairs), units)


def on_even(even, odd):
    is_even = lax.axis_index("seq") % 2 == 0
    units = odd.units.copy()
    units[::2] = even.units[::2]
    return Piece(jnp.where(is_even, even.array, odd.array), units)


def cube_exchange(own):
    chip = lambda c, b: 2 * c + b
    both = (0, 1)
    low, high = own.rows(0, 1), own.rows(1, 2)
    beside = own.to([(chip(c, 0), chip(c, 1)) for c in range(4)])
    near = own.to([(chip(c, b), chip(c + 1, b)) for c in (0, 2) for b in both])
    far_low = low.to(
        [(chip(0, 1), chip(2, 0)), (chip(1, 1), chip(3, 0)), (chip(1, 0), chip(2, 1))]
    )
    far_high = high.to([(chip(c, b), chip(c + 2, b)) for c in (0, 1) for b in both])
    on_low = far_low.to([(chip(3, 0), chip(2, 0))])
    on_high = far_high.to([(chip(3, b), chip(2, b)) for b in both])
    swap = lambda *chips: [(chip(c, b), chip(c, 1 - b)) for c in chips for b in both]
    return [
        own,
        beside,
        near,
        far_low,
        far_high,
        on_low,
        on_high,
        far_high.to([(chip(c, 1), chip(c, 0)) for c in (2, 3)]),
        near.to(swap(1, 3)),
        on_high.to(swap(2)),
        on_even(on_low, far_low).to(swap(2)),
    ]


def gather_exchange(own):
    count, each = own.units.shape
    everything = lax.all_gather(own.array, "seq", axis=0, tiled=True)
    return [Piece(everything, np.tile(np.arange(count * each), (count, 1)))]


def slots_of(pieces, window, each):
    slots, table = [], []
    count = pieces[0].units.shape[0]
    held = [set() for _ in range(count)]
    for number, piece in enumerate(pieces):
        for block in range(piece.units.shape[1]):
            column = []
            for device in range(count):
                unit = int(piece.units[device, block])
                last = each * device + each - 1
                fits = last - window < unit <= last and unit >= 0 and unit not in held[device]
                column.append(unit if fits else -1)
                if fits:
                    held[device].add(unit)
            if max(column) >= 0:
                slots.append((number, block))
                table.append(column)
    for device in range(count):
        last = each * device + each - 1
        assert held[device] == set(range(max(0, last - window + 1), last + 1))
    return slots, np.array(table, np.int32).T


def attend_kernel(plan, table_ref, docs_ref, q_ref, *refs):
    slots, n_pieces, window, each, group, width, n_docs = plan
    pieces, out_ref, (buf, sems, state_m, state_l, state_o) = (
        refs[:n_pieces],
        refs[-6],
        refs[-5:],
    )
    device = lax.axis_index("seq")
    head = pl.program_id(0)
    first_unit = device * each
    base = first_unit + each - window

    def doc_start(unit):
        start, passed = jnp.int32(0), jnp.int32(0)
        for d in range(n_docs):
            passed = passed + docs_ref[d]
            start = jnp.where(passed <= unit, passed, start)
        return start

    lowest_unit = doc_start(first_unit)

    @pl.when(head == 0)
    def _():
        def each_copy(act):
            for t, (number, block) in enumerate(slots):
                unit = table_ref[device * len(slots) + t]

                @pl.when(unit >= lowest_unit)
                def _():
                    place = pl.multiple_of((unit - base) * DOC_UNIT, DOC_UNIT)
                    act(
                        pltpu.make_async_copy(
                            pieces[number].at[pl.ds(block * DOC_UNIT, DOC_UNIT)],
                            buf.at[pl.ds(place, DOC_UNIT)],
                            sems.at[t],
                        )
                    )

        each_copy(lambda copy: copy.start())
        each_copy(lambda copy: copy.wait())

    factor = HEAD_DIM**-0.5 * math.log2(math.e)
    key_columns = pl.ds(pl.multiple_of(head * HEAD_DIM, HEAD_DIM), HEAD_DIM)
    value_columns = pl.ds(pl.multiple_of(width + head * HEAD_DIM, HEAD_DIM), HEAD_DIM)
    rows = group * DOC_UNIT

    def stacked(part):
        q = q_ref[pl.ds(pl.multiple_of(part * DOC_UNIT, DOC_UNIT), DOC_UNIT), :]
        return jnp.concatenate(
            [q[:, g * HEAD_DIM : (g + 1) * HEAD_DIM] for g in range(group)], axis=0
        )

    def scores_of(q, first, units):
        key_rows = buf[pl.ds(pl.multiple_of(first * DOC_UNIT, DOC_UNIT), units * DOC_UNIT), key_columns]
        return lax.dot_general(
            q, key_rows, (((1,), (1,)), ((), ())), preferred_element_type=jnp.float32
        )

    def mixed(weights, first, units):
        value_rows = buf[pl.ds(pl.multiple_of(first * DOC_UNIT, DOC_UNIT), units * DOC_UNIT), value_columns]
        return jnp.dot(
            weights.astype(jnp.bfloat16), value_rows, preferred_element_type=jnp.float32
        )

    def store(part, result):
        for g in range(group):
            out_ref[
                pl.ds(pl.multiple_of(part * DOC_UNIT, DOC_UNIT), DOC_UNIT),
                g * HEAD_DIM : (g + 1) * HEAD_DIM,
            ] = result[g * DOC_UNIT : (g + 1) * DOC_UNIT].astype(out_ref.dtype)

    most = min(MOST_UNITS, window - each + 1)
    longer = window - each + 1 > most

    def each_part(part, carry):
        unit = first_unit + part
        start = doc_start(unit)
        count = unit - start + 1
        here = lax.rem(count - 1, most) + 1
        for units in range(1, most + 1):

            @pl.when(here == units)
            def _():
                first = unit - base - units + 1
                q = stacked(part)
                scores = scores_of(q, first, units)
                last = scores[:, (units - 1) * DOC_UNIT :]
                row = lax.broadcasted_iota(jnp.int32, last.shape, 0) % DOC_UNIT
                column = lax.broadcasted_iota(jnp.int32, last.shape, 1)
                last = jnp.where(column <= row, last, -jnp.inf)
                if units > 1:
                    scores = jnp.concatenate([scores[:, : (units - 1) * DOC_UNIT], last], axis=1)
                else:
                    scores = last
                top = jnp.max(scores, axis=1, keepdims=True)
                weights = jnp.exp2((scores - top) * factor)
                total = jnp.sum(weights, axis=1, keepdims=True)
                result = mixed(weights, first, units)
                if longer:
                    state_m[...], state_l[...], state_o[...] = top, total, result
                else:
                    store(part, result / total)

        if longer:
            q = stacked(part)

            def add_block(number, carry):
                first = start - base + number * most
                scores = scores_of(q, first, most)
                old = state_m[...]
                top = jnp.maximum(old, jnp.max(scores, axis=1, keepdims=True))
                weights = jnp.exp2((scores - top) * factor)
                shrink = jnp.exp2((old - top) * factor)
                state_m[...] = top
                state_l[...] = state_l[...] * shrink + jnp.sum(weights, axis=1, keepdims=True)
                state_o[...] = state_o[...] * shrink + mixed(weights, first, most)
                return carry

            lax.fori_loop(0, lax.div(count - 1, most), add_block, 0)
            store(part, state_o[...] / state_l[...])
        return carry

    lax.fori_loop(0, each, each_part, 0)


def attend(queries, doc_lengths, pieces, window, each, group, first_head, heads, before):
    slots, table = slots_of(pieces, window, each)
    width = heads * HEAD_DIM
    rows = each * DOC_UNIT
    columns = group * HEAD_DIM
    plan = (slots, len(pieces), window, each, group, width, doc_lengths.shape[0])
    anywhere = pl.BlockSpec(memory_space=pl.ANY)
    block = pl.BlockSpec((rows, columns), lambda h, *_: (0, first_head + h))
    extra = [] if before is None else [before]
    work = window * DOC_UNIT * rows * heads * group * HEAD_DIM * 2
    n_long = group * DOC_UNIT if window - each + 1 > MOST_UNITS else 8
    return pl.pallas_call(
        functools.partial(attend_kernel, plan),
        out_shape=jax.ShapeDtypeStruct(queries.shape, queries.dtype),
        grid_spec=pltpu.PrefetchScalarGridSpec(
            num_scalar_prefetch=2,
            grid=(heads,),
            in_specs=[block] + [anywhere] * (len(pieces) + len(extra)),
            out_specs=block,
            scratch_shapes=[
                pltpu.VMEM((window * DOC_UNIT, 2 * width), queries.dtype),
                pltpu.SemaphoreType.DMA((len(slots),)),
                pltpu.VMEM((n_long, 1), jnp.float32),
                pltpu.VMEM((n_long, 1), jnp.float32),
                pltpu.VMEM((n_long, HEAD_DIM), jnp.float32),
            ],
        ),
        input_output_aliases={} if before is None else {3 + len(pieces): 0},
        cost_estimate=pl.CostEstimate(
            flops=work,
            transcendentals=work // (4 * HEAD_DIM),
            bytes_accessed=2 * rows * columns * heads * 2 + window * DOC_UNIT * width * 4,
        ),
    )(jnp.asarray(table.reshape(-1)), doc_lengths, queries, *[p.array for p in pieces], *extra)


def on_device(queries, keys, values, doc_lengths):
    rows = queries.shape[0]
    kv_heads = keys.shape[1] // HEAD_DIM
    group = queries.shape[1] // keys.shape[1]
    count = lax.axis_size("seq")
    each = rows // DOC_UNIT
    longest = count * each // 2
    window = longest - 1 + each
    exchange = cube_exchange if (count, each) == (8, 2) else gather_exchange
    out = None
    parts = PARTS_OF_HEADS
    for part in range(parts):
        first, last = kv_heads * part // parts, kv_heads * (part + 1) // parts
        columns = slice(first * HEAD_DIM, last * HEAD_DIM)
        both = jnp.concatenate([keys[:, columns], values[:, columns]], axis=1)
        own = Piece(both, np.arange(count * each).reshape(count, each))
        pieces = exchange(own)
        out = attend(
            queries, doc_lengths, pieces, window, each, group, first, last - first, out
        )
    return out


def solution(mesh):
    rows = P(("grp", "seq"), None)
    return jax.shard_map(
        on_device, mesh=mesh, in_specs=(rows, rows, rows, P("grp")), out_specs=rows, check_vma=False
    )
```

```python
import functools
import math

import jax
import jax.numpy as jnp
import numpy as np
from jax import lax
from jax.experimental import pallas as pl
from jax.experimental.pallas import tpu as pltpu
from jax.sharding import PartitionSpec as P


HEAD_DIM = 128
DOC_UNIT = 128
MOST_UNITS = 8
PARTS_OF_HEADS = 2


class Piece:
    def __init__(self, array, units):
        self.array, self.units = array, units

    def rows(self, first, last):
        return Piece(self.array[first * DOC_UNIT : last * DOC_UNIT], self.units[:, first:last])

    def to(self, pairs):
        units = np.full_like(self.units, -1)
        for source, target in pairs:
            units[target] = self.units[source]
        return Piece(lax.ppermute(self.array, "seq", pairs), units)


def cube_exchange(low, high):
    chip = lambda c, b: 2 * c + b
    both = (0, 1)
    swap = lambda *chips: [(chip(c, b), chip(c, 1 - b)) for c in chips for b in both]
    next_chip = [(chip(c, b), chip(c + 1, b)) for c in (0, 2) for b in both]
    beside = [(chip(c, 0), chip(c, 1)) for c in range(4)]
    a_low = low.to([(chip(1, 1), chip(3, 0))])
    a_high = high.to([(chip(1, b), chip(3, b)) for b in both])
    b_low = low.to([(chip(0, 1), chip(2, 0)), (chip(1, 0), chip(2, 1))])
    b_high = high.to([(chip(0, b), chip(2, b)) for b in both])
    near_low, near_high = low.to(next_chip), high.to(next_chip)
    on_low = a_low.to([(chip(3, 0), chip(2, 0))])
    on_high = a_high.to([(chip(3, b), chip(2, b)) for b in both])
    first = [
        low,
        high,
        low.to(beside),
        high.to(beside),
        a_low,
        a_high,
        b_low,
        b_high,
        near_low,
        on_low,
        near_low.to(swap(1, 3)),
        on_low.to([(chip(2, 0), chip(2, 1))]),
        b_low.to([(chip(2, 1), chip(2, 0))]),
        b_high.to([(chip(2, 1), chip(2, 0))]),
        a_high.to([(chip(3, 1), chip(3, 0))]),
    ]
    last = [near_high, on_high, near_high.to(swap(1, 3)), on_high.to(swap(2))]
    return first, last


def gather_exchange(own):
    count, each = own.units.shape
    everything = lax.all_gather(own.array, "seq", axis=0, tiled=True)
    return [Piece(everything, np.tile(np.arange(count * each), (count, 1)))]


def slots_of(pieces, window, each, wanted=lambda device, unit: True):
    slots, table = [], []
    count = pieces[0].units.shape[0]
    held = [set() for _ in range(count)]
    for number, piece in enumerate(pieces):
        for block in range(piece.units.shape[1]):
            column = []
            for device in range(count):
                unit = int(piece.units[device, block])
                last = each * device + each - 1
                fits = last - window < unit <= last and unit >= 0 and unit not in held[device]
                column.append(unit if fits else -1)
                if fits:
                    held[device].add(unit)
            if max(column) >= 0:
                slots.append((number, block))
                table.append(column)
    for device in range(count):
        last = each * device + each - 1
        units = range(max(0, last - window + 1), last + 1)
        assert held[device] == {unit for unit in units if wanted(device, unit)}
    return slots, np.array(table, np.int32).T


def doc_start(docs_ref, unit):
    start, passed = jnp.int32(0), jnp.int32(0)
    for d in range(docs_ref.shape[0]):
        passed = passed + docs_ref[d]
        start = jnp.where(passed <= unit, passed, start)
    return start


def held_unit(column, device):
    held = set(column.tolist()) - {-1}
    if len(held) == 1 and (column >= 0).all():
        return jnp.int32(held.pop())
    unit = jnp.int32(-1)
    for holder in np.flatnonzero(column >= 0):
        unit = jnp.where(device == int(holder), int(column[holder]), unit)
    return unit


FACTOR = HEAD_DIM**-0.5 * math.log2(math.e)


def rows_of(first, units):
    return pl.ds(pl.multiple_of(first * DOC_UNIT, DOC_UNIT), units * DOC_UNIT)


def columns_of(head, width=HEAD_DIM):
    return pl.ds(pl.multiple_of(head * width, width), width)


def stacked(q, heads):
    return jnp.concatenate([q[:, g * HEAD_DIM : (g + 1) * HEAD_DIM] for g in heads], axis=0)


def scores_of(q, key_rows):
    return lax.dot_general(
        q, key_rows, (((1,), (1,)), ((), ())), preferred_element_type=jnp.float32
    )


def mixed(weights, value_rows):
    ones = jnp.ones(value_rows.shape, value_rows.dtype)
    return jnp.dot(
        weights.astype(value_rows.dtype),
        jnp.concatenate([value_rows, ones], axis=1),
        preferred_element_type=jnp.float32,
    )


def masked_last(scores, units):
    last = scores[:, (units - 1) * DOC_UNIT :]
    row = lax.broadcasted_iota(jnp.int32, last.shape, 0) % DOC_UNIT
    column = lax.broadcasted_iota(jnp.int32, last.shape, 1)
    last = jnp.where(column <= row, last, -jnp.inf)
    if units == 1:
        return last
    return jnp.concatenate([scores[:, : (units - 1) * DOC_UNIT], last], axis=1)


def twice(tile):
    return jnp.concatenate([tile, tile], axis=1)


def in_turn(jobs, start, finish):
    pending = start(jobs[0])
    for number, job in enumerate(jobs):
        started = pending
        if number + 1 < len(jobs):
            pending = start(jobs[number + 1])
        finish(job, started)


CHUNK = 2
AT_ONCE = 2


def unit_copies(pieces, slots, table, sems, buf, device, lowest, place):
    def each_copy(act):
        for t, (number, block) in enumerate(slots):
            unit = held_unit(table[:, t], device)

            @pl.when(unit >= lowest)
            def _():
                act(
                    pltpu.make_async_copy(
                        pieces[number].at[pl.ds(block * DOC_UNIT, DOC_UNIT)],
                        buf.at[rows_of(place(unit), 1)],
                        sems.at[t],
                    )
                )

    return each_copy


def late_units(device):
    chip = device >> 1
    return 4 * chip - 3, 4 * chip - 1


def first_kernel(plan, docs_ref, q_hbm, *refs):
    slots, table, n_pieces, window, each, group, heads = plan
    pieces = refs[:n_pieces]
    mixed_ref, top_ref, q_all, buf, sems, q_sem = refs[n_pieces:]
    device = lax.axis_index("seq")
    first_unit = device * each
    base = first_unit + each - window
    late = late_units(device)
    columns = group * HEAD_DIM

    def place(unit):
        return unit - base - (unit > late[0]).astype(jnp.int32) - (unit > late[1]).astype(jnp.int32)

    each_copy = unit_copies(
        pieces, slots, table, sems, buf, device, doc_start(docs_ref, first_unit), place
    )
    q_copy = pltpu.make_async_copy(q_hbm, q_all, q_sem)
    each_copy(lambda copy: copy.start())
    q_copy.start()
    each_copy(lambda copy: copy.wait())
    q_copy.wait()

    def one_step(step, carry):
        pair, part = lax.div(step, each), lax.rem(step, each)
        unit = first_unit + part
        start = doc_start(docs_ref, unit)
        skipped = sum(((u >= start) & (u <= unit)).astype(jnp.int32) for u in late)
        here = unit - start + 1 - skipped
        for units in range(1, window - each):

            @pl.when(here == units)
            def _():
                rows = rows_of(place(unit) - units + 1, units)
                jobs = [(h, g) for h in range(AT_ONCE) for g in range(0, group, CHUNK)]

                def begin(job):
                    head, g = pair * AT_ONCE + job[0], job[1]
                    q = q_all[rows_of(part, 1), columns_of(head, columns)]
                    keys = buf[rows, columns_of(head)]
                    return scores_of(stacked(q, range(g, g + CHUNK)), keys)

                def end(job, scores):
                    h, g = job
                    head = pair * AT_ONCE + h
                    scores = masked_last(scores, units)
                    top = jnp.max(scores, axis=1, keepdims=True)
                    weights = jnp.exp2((scores - top) * FACTOR)
                    mine = pl.ds(g * DOC_UNIT, CHUNK * DOC_UNIT)
                    mixed_ref[step, h, mine] = mixed(weights, buf[rows, columns_of(heads + head)])
                    top_ref[step, h, mine] = jnp.broadcast_to(top, (CHUNK * DOC_UNIT, HEAD_DIM))

                in_turn(jobs, begin, end)

        return carry

    lax.fori_loop(0, heads // AT_ONCE * each, one_step, 0)


def last_kernel(plan, docs_ref, q_hbm, mixed_ref, top_ref, *refs):
    slots, table, n_pieces, _, each, group, heads = plan
    pieces = refs[:n_pieces]
    out_hbm, q_all, buf, out_all, sems, q_sem, out_sems = refs[n_pieces:]
    device = lax.axis_index("seq")
    first_unit = device * each
    late = late_units(device)
    columns = group * HEAD_DIM
    steps = heads // AT_ONCE * each

    place = lambda unit: (unit > late[0]).astype(jnp.int32)
    each_copy = unit_copies(pieces, slots, table, sems, buf, device, 0, place)
    q_copy = pltpu.make_async_copy(q_hbm, q_all, q_sem)

    def copy_out(pair):
        there = columns_of(pair, AT_ONCE * columns)
        return pltpu.make_async_copy(out_all.at[:, there], out_hbm.at[:, there], out_sems.at[pair])

    each_copy(lambda copy: copy.start())
    q_copy.start()
    each_copy(lambda copy: copy.wait())
    q_copy.wait()

    def one_step(step, carry):
        pair, part = lax.div(step, each), lax.rem(step, each)
        unit = first_unit + part
        start = doc_start(docs_ref, unit)
        count = sum((u >= start).astype(jnp.int32) for u in late)
        jobs = [(h, g) for h in range(AT_ONCE) for g in range(0, group, CHUNK)]

        def older(ref, job):
            return ref[step, job[0], pl.ds(job[1] * DOC_UNIT, CHUNK * DOC_UNIT)]

        def mean(result):
            return result[:, :HEAD_DIM] / result[:, HEAD_DIM:]

        def store(job, rows):
            for k in range(CHUNK):
                head = (pair * AT_ONCE + job[0]) * group + job[1] + k
                out_all[rows_of(part, 1), columns_of(head)] = rows[
                    k * DOC_UNIT : (k + 1) * DOC_UNIT
                ].astype(out_all.dtype)

        @pl.when(count == 0)
        def _():
            for job in jobs:
                store(job, mean(older(mixed_ref, job)))

        @pl.when(count > 0)
        def _():
            def begin(job):
                head = pair * AT_ONCE + job[0]
                q = q_all[rows_of(part, 1), columns_of(head, columns)]
                return scores_of(stacked(q, range(job[1], job[1] + CHUNK)), buf[:, columns_of(head)])

            def end(job, scores):
                head = pair * AT_ONCE + job[0]
                column = lax.broadcasted_iota(jnp.int32, scores.shape, 1)
                scores = jnp.where(column >= (2 - count) * DOC_UNIT, scores, -jnp.inf)
                old = older(top_ref, job)
                top = jnp.maximum(old, jnp.max(scores, axis=1, keepdims=True))
                weights = jnp.exp2((scores - twice(top)) * FACTOR)
                shrink = jnp.exp2((old - top) * FACTOR)
                result = mixed(weights, buf[:, columns_of(heads + head)])
                store(job, mean(older(mixed_ref, job) * twice(shrink) + result))

            in_turn(jobs, begin, end)

        @pl.when(part == each - 1)
        def _():
            copy_out(pair).start()

        return carry

    lax.fori_loop(0, steps, one_step, 0)
    for pair in range(heads // AT_ONCE):
        copy_out(pair).wait()


def in_two(queries, doc_lengths, first, last, window, each, group, heads):
    rows = each * DOC_UNIT
    dtype = queries.dtype
    steps = heads // AT_ONCE * each
    anywhere = pl.BlockSpec(memory_space=pl.ANY)
    dma = pltpu.SemaphoreType.DMA
    tile = (steps, AT_ONCE, group * DOC_UNIT, HEAD_DIM)
    state = (
        pltpu.VMEM((*tile[:-1], 2 * HEAD_DIM), jnp.float32),
        pltpu.VMEM(tile, jnp.float32),
    )
    on_chip = pl.BlockSpec(memory_space=pltpu.VMEM)
    is_late = lambda device, unit: unit in late_units(device)

    def call(kernel, pieces, wanted, held_rows, operands, in_specs, shapes, out_specs, scratch):
        slots, table = slots_of(pieces, window, each, wanted)
        plan = (slots, table, len(pieces), window, each, group, heads)
        scratch = [
            pltpu.VMEM(queries.shape, dtype),
            pltpu.VMEM((held_rows, 2 * heads * HEAD_DIM), dtype),
            *scratch(len(slots)),
        ]
        work = held_rows * rows * heads * group * HEAD_DIM * 2
        return pl.pallas_call(
            functools.partial(kernel, plan),
            out_shape=shapes,
            grid_spec=pltpu.PrefetchScalarGridSpec(
                num_scalar_prefetch=1,
                grid=(),
                in_specs=[*in_specs, *[anywhere] * len(pieces)],
                out_specs=out_specs,
                scratch_shapes=scratch,
            ),
            compiler_params=pltpu.CompilerParams(vmem_limit_bytes=VMEM_LIMIT),
            cost_estimate=pl.CostEstimate(
                flops=work, transcendentals=work // (4 * HEAD_DIM), bytes_accessed=4 * queries.size * 2
            ),
        )(doc_lengths, *operands, *[p.array for p in pieces])

    so_far = call(
        first_kernel,
        first,
        lambda device, unit: not is_late(device, unit),
        (window - 2) * DOC_UNIT,
        (queries,),
        (anywhere,),
        state,
        (on_chip, on_chip),
        lambda n: [dma((n,)), dma],
    )
    return call(
        last_kernel,
        last,
        is_late,
        2 * DOC_UNIT,
        (queries, *so_far),
        (anywhere, on_chip, on_chip),
        jax.ShapeDtypeStruct(queries.shape, dtype),
        anywhere,
        lambda n: [pltpu.VMEM(queries.shape, dtype), dma((n,)), dma, dma((heads // AT_ONCE,))],
    )


VMEM_LIMIT = 24 << 20


def attend_kernel(plan, docs_ref, q_hbm, *refs):
    slots, table, n_pieces, window, each, group, first_head, heads, n_docs = plan
    pieces, out_hbm = refs[:n_pieces], refs[-9]
    q_all, out_all, buf, sems, q_sems, out_sems, state_m, state_o = refs[-8:]
    device = lax.axis_index("seq")
    first_unit = device * each
    base = first_unit + each - window
    width = heads * HEAD_DIM
    columns = group * HEAD_DIM

    def doc_start(unit):
        start, passed = jnp.int32(0), jnp.int32(0)
        for d in range(n_docs):
            passed = passed + docs_ref[d]
            start = jnp.where(passed <= unit, passed, start)
        return start

    lowest_unit = doc_start(first_unit)

    def each_copy(act):
        for t, (number, block) in enumerate(slots):
            held = set(table[:, t].tolist()) - {-1}
            if len(held) == 1:
                unit = jnp.int32(held.pop())
            else:
                unit = jnp.int32(-1)
                for holder in np.flatnonzero(table[:, t] >= 0):
                    unit = jnp.where(device == int(holder), int(table[holder, t]), unit)

            @pl.when((unit >= lowest_unit) & (unit < first_unit + each))
            def _():
                place = pl.multiple_of((unit - base) * DOC_UNIT, DOC_UNIT)
                act(
                    pltpu.make_async_copy(
                        pieces[number].at[pl.ds(block * DOC_UNIT, DOC_UNIT)],
                        buf.at[pl.ds(place, DOC_UNIT)],
                        sems.at[t],
                    )
                )

    def q_copy(head):
        there = pl.ds(pl.multiple_of((first_head + head) * columns, columns), columns)
        return pltpu.make_async_copy(q_hbm.at[:, there], q_all.at[head], q_sems.at[head])

    def out_copy(head):
        there = pl.ds(pl.multiple_of((first_head + head) * columns, columns), columns)
        return pltpu.make_async_copy(out_all.at[head], out_hbm.at[:, there], out_sems.at[head])

    q_copy(0).start()
    each_copy(lambda copy: copy.start())
    for head in range(1, heads):
        q_copy(head).start()
    each_copy(lambda copy: copy.wait())

    factor = HEAD_DIM**-0.5 * math.log2(math.e)
    ones = jnp.ones((min(MOST_UNITS, window) * DOC_UNIT, HEAD_DIM), buf.dtype)
    most = min(MOST_UNITS, window - each + 1)
    longer = window - each + 1 > most

    def each_head(head, carry):
        q_copy(head).wait()
        key_columns = pl.ds(pl.multiple_of(head * HEAD_DIM, HEAD_DIM), HEAD_DIM)
        value_columns = pl.ds(pl.multiple_of(width + head * HEAD_DIM, HEAD_DIM), HEAD_DIM)

        def stacked(part):
            q = q_all[head, pl.ds(part * DOC_UNIT, DOC_UNIT), :]
            return jnp.concatenate(
                [q[:, g * HEAD_DIM : (g + 1) * HEAD_DIM] for g in range(group)], axis=0
            )

        def scores_of(q, first, units):
            there = pl.ds(pl.multiple_of(first * DOC_UNIT, DOC_UNIT), units * DOC_UNIT)
            return lax.dot_general(
                q, buf[there, key_columns], (((1,), (1,)), ((), ())), preferred_element_type=jnp.float32
            )

        def mixed(weights, first, units):
            there = pl.ds(pl.multiple_of(first * DOC_UNIT, DOC_UNIT), units * DOC_UNIT)
            value_rows = jnp.concatenate([buf[there, value_columns], ones[: units * DOC_UNIT]], axis=1)
            return jnp.dot(
                weights.astype(buf.dtype), value_rows, preferred_element_type=jnp.float32
            )

        def store(part, result):
            result = result[:, :HEAD_DIM] / result[:, HEAD_DIM:]
            for g in range(group):
                out_all[
                    head, pl.ds(part * DOC_UNIT, DOC_UNIT), g * HEAD_DIM : (g + 1) * HEAD_DIM
                ] = result[g * DOC_UNIT : (g + 1) * DOC_UNIT].astype(out_all.dtype)

        for part in range(each):
            unit = first_unit + part
            start = doc_start(unit)
            count = unit - start + 1
            here = lax.rem(count - 1, most) + 1
            for units in range(1, most + 1):

                @pl.when(here == units)
                def _():
                    first = unit - base - units + 1
                    scores = scores_of(stacked(part), first, units)
                    last = scores[:, (units - 1) * DOC_UNIT :]
                    row = lax.broadcasted_iota(jnp.int32, last.shape, 0) % DOC_UNIT
                    column = lax.broadcasted_iota(jnp.int32, last.shape, 1)
                    last = jnp.where(column <= row, last, -jnp.inf)
                    if units > 1:
                        before = scores[:, : (units - 1) * DOC_UNIT]
                        scores = jnp.concatenate([before, last], axis=1)
                    else:
                        scores = last
                    top = jnp.max(scores, axis=1, keepdims=True)
                    result = mixed(jnp.exp2((scores - top) * factor), first, units)
                    if longer:
                        state_m[...], state_o[...] = top, result
                    else:
                        store(part, result)

            if longer:

                def add_block(number, carry):
                    first = start - base + number * most
                    scores = scores_of(stacked(part), first, most)
                    old = state_m[...]
                    top = jnp.maximum(old, jnp.max(scores, axis=1, keepdims=True))
                    weights = jnp.exp2((scores - top) * factor)
                    shrink = jnp.exp2((old - top) * factor)
                    state_m[...] = top
                    state_o[...] = state_o[...] * shrink + mixed(weights, first, most)
                    return carry

                lax.fori_loop(0, lax.div(count - 1, most), add_block, 0)
                store(part, state_o[...])
        out_copy(head).start()
        return carry

    lax.fori_loop(0, heads, each_head, 0)
    for head in range(heads):
        out_copy(head).wait()


def attend(queries, doc_lengths, pieces, window, each, group, first_head, heads, before):
    slots, table = slots_of(pieces, window, each)
    width = heads * HEAD_DIM
    rows = each * DOC_UNIT
    columns = group * HEAD_DIM
    plan = (slots, table, len(pieces), window, each, group, first_head, heads, doc_lengths.shape[0])
    anywhere = pl.BlockSpec(memory_space=pl.ANY)
    extra = [] if before is None else [before]
    work = window * DOC_UNIT * rows * heads * group * HEAD_DIM * 2
    n_long = group * DOC_UNIT if window - each + 1 > MOST_UNITS else 8
    held = (window * DOC_UNIT * 2 * width + 2 * rows * columns * heads) * 2
    return pl.pallas_call(
        functools.partial(attend_kernel, plan),
        out_shape=jax.ShapeDtypeStruct(queries.shape, queries.dtype),
        grid_spec=pltpu.PrefetchScalarGridSpec(
            num_scalar_prefetch=1,
            grid=(),
            in_specs=[anywhere] * (1 + len(pieces) + len(extra)),
            out_specs=anywhere,
            scratch_shapes=[
                pltpu.VMEM((heads, rows, columns), queries.dtype),
                pltpu.VMEM((heads, rows, columns), queries.dtype),
                pltpu.VMEM((window * DOC_UNIT, 2 * width), queries.dtype),
                pltpu.SemaphoreType.DMA((len(slots),)),
                pltpu.SemaphoreType.DMA((heads,)),
                pltpu.SemaphoreType.DMA((heads,)),
                pltpu.VMEM((n_long, 1), jnp.float32),
                pltpu.VMEM((n_long, 2 * HEAD_DIM), jnp.float32),
            ],
        ),
        input_output_aliases={} if before is None else {2 + len(pieces): 0},
        compiler_params=pltpu.CompilerParams(vmem_limit_bytes=held + (12 << 20)),
        cost_estimate=pl.CostEstimate(
            flops=work,
            transcendentals=work // (4 * HEAD_DIM),
            bytes_accessed=2 * rows * columns * heads * 2 + window * DOC_UNIT * width * 4,
        ),
    )(doc_lengths, queries, *[p.array for p in pieces], *extra)


def on_device(queries, keys, values, doc_lengths):
    rows = queries.shape[0]
    heads = keys.shape[1] // HEAD_DIM
    group = queries.shape[1] // keys.shape[1]
    count = lax.axis_size("seq")
    each = rows // DOC_UNIT
    longest = count * each // 2
    window = longest - 1 + each
    units = np.arange(count * each).reshape(count, each)
    if is_cube(count, each):
        low, high = (
            Piece(jnp.concatenate([keys[part], values[part]], axis=1), units[:, u : u + 1])
            for u, part in enumerate((slice(0, DOC_UNIT), slice(DOC_UNIT, rows)))
        )
        first, last = cube_exchange(low, high)
        return in_two(queries, doc_lengths, first, last, window, each, group, heads)
    out = None
    parts = PARTS_OF_HEADS
    for part in range(parts):
        first, last = heads * part // parts, heads * (part + 1) // parts
        columns = slice(first * HEAD_DIM, last * HEAD_DIM)
        both = jnp.concatenate([keys[:, columns], values[:, columns]], axis=1)
        pieces = gather_exchange(Piece(both, units))
        out = attend(
            queries, doc_lengths, pieces, window, each, group, first, last - first, out
        )
    return out


def is_cube(count, each):
    return (count, each) == (8, 2)


def solution(mesh):
    rows = P(("grp", "seq"), None)
    return jax.shard_map(
        on_device, mesh=mesh, in_specs=(rows, rows, rows, P("grp")), out_specs=rows, check_vma=False
    )
```

```python
import functools
import math

import jax
import jax.numpy as jnp
import numpy as np
from jax import lax
from jax.experimental import pallas as pl
from jax.experimental.pallas import tpu as pltpu
from jax.sharding import PartitionSpec as P


HEAD_DIM = 128
DOC_UNIT = 128
MOST_UNITS = 8
PARTS_OF_HEADS = 2


class Piece:
    def __init__(self, array, units):
        self.array, self.units = array, units

    def rows(self, first, last):
        return Piece(self.array[first * DOC_UNIT : last * DOC_UNIT], self.units[:, first:last])

    def to(self, pairs):
        units = np.full_like(self.units, -1)
        for source, target in pairs:
            units[target] = self.units[source]
        return Piece(lax.ppermute(self.array, "seq", pairs), units)


def cube_exchange(low, high):
    chip = lambda c, b: 2 * c + b
    both = (0, 1)
    swap = lambda *chips: [(chip(c, b), chip(c, 1 - b)) for c in chips for b in both]
    next_chip = [(chip(c, b), chip(c + 1, b)) for c in (0, 2) for b in both]
    beside = [(chip(c, 0), chip(c, 1)) for c in range(4)]
    b_low = low.to([(chip(0, 1), chip(2, 0))])
    b_high = high.to([(chip(0, b), chip(2, b)) for b in both])
    near_low = low.to([*next_chip, (chip(1, 0), chip(2, 1))])
    near_high = high.to(next_chip)
    a_low = low.to([(chip(1, 1), chip(3, 0))])
    a_high = high.to([(chip(1, b), chip(3, b)) for b in both])
    on_low = a_low.to([(chip(3, 0), chip(2, 0))])
    on_high = a_high.to([(chip(3, b), chip(2, b)) for b in both])
    first = [
        low,
        high,
        low.to(beside),
        high.to(beside),
        a_low,
        a_high,
        b_low,
        b_high,
        near_low,
        on_low,
        near_low.to([*swap(1, 3), (chip(2, 1), chip(2, 0))]),
        on_low.to([(chip(2, 0), chip(2, 1))]),
        b_high.to([(chip(2, 1), chip(2, 0))]),
        a_high.to([(chip(3, 1), chip(3, 0))]),
    ]
    last = [near_high, on_high, near_high.to(swap(1, 3)), on_high.to(swap(2))]
    return first, last


def gather_exchange(own):
    count, each = own.units.shape
    everything = lax.all_gather(own.array, "seq", axis=0, tiled=True)
    return [Piece(everything, np.tile(np.arange(count * each), (count, 1)))]


def slots_of(pieces, window, each, wanted=lambda device, unit: True):
    slots, table = [], []
    count = pieces[0].units.shape[0]
    held = [set() for _ in range(count)]
    for number, piece in enumerate(pieces):
        for block in range(piece.units.shape[1]):
            column = []
            for device in range(count):
                unit = int(piece.units[device, block])
                last = each * device + each - 1
                fits = last - window < unit <= last and unit >= 0 and unit not in held[device]
                column.append(unit if fits else -1)
                if fits:
                    held[device].add(unit)
            if max(column) >= 0:
                slots.append((number, block))
                table.append(column)
    for device in range(count):
        last = each * device + each - 1
        units = range(max(0, last - window + 1), last + 1)
        assert held[device] == {unit for unit in units if wanted(device, unit)}
    return slots, np.array(table, np.int32).T


def doc_start(docs_ref, unit):
    start, passed = jnp.int32(0), jnp.int32(0)
    for d in range(docs_ref.shape[0]):
        passed = passed + docs_ref[d]
        start = jnp.where(passed <= unit, passed, start)
    return start


def held_unit(column, device):
    held = set(column.tolist()) - {-1}
    if len(held) == 1 and (column >= 0).all():
        return jnp.int32(held.pop())
    unit = jnp.int32(-1)
    for holder in np.flatnonzero(column >= 0):
        unit = jnp.where(device == int(holder), int(column[holder]), unit)
    return unit


FACTOR = HEAD_DIM**-0.5 * math.log2(math.e)


def rows_of(first, units):
    return pl.ds(pl.multiple_of(first * DOC_UNIT, DOC_UNIT), units * DOC_UNIT)


def columns_of(head, width=HEAD_DIM):
    return pl.ds(pl.multiple_of(head * width, width), width)


def stacked(q, heads):
    return jnp.concatenate([q[:, g * HEAD_DIM : (g + 1) * HEAD_DIM] for g in heads], axis=0)


def scores_of(q, key_rows):
    return lax.dot_general(
        q, key_rows, (((1,), (1,)), ((), ())), preferred_element_type=jnp.float32
    )


def mixed(weights, value_rows):
    ones = jnp.ones(value_rows.shape, value_rows.dtype)
    return jnp.dot(
        weights.astype(value_rows.dtype),
        jnp.concatenate([value_rows, ones], axis=1),
        preferred_element_type=jnp.float32,
    )


def masked_last(scores, units):
    last = scores[:, (units - 1) * DOC_UNIT :]
    row = lax.broadcasted_iota(jnp.int32, last.shape, 0) % DOC_UNIT
    column = lax.broadcasted_iota(jnp.int32, last.shape, 1)
    last = jnp.where(column <= row, last, -jnp.inf)
    if units == 1:
        return last
    return jnp.concatenate([scores[:, : (units - 1) * DOC_UNIT], last], axis=1)


def twice(tile):
    return jnp.concatenate([tile, tile], axis=1)


def in_turn(jobs, start, finish):
    pending = start(jobs[0])
    for number, job in enumerate(jobs):
        started = pending
        if number + 1 < len(jobs):
            pending = start(jobs[number + 1])
        finish(job, started)


CHUNK = 2
FIRST_HEADS, LAST_HEADS = 4, 8


def unit_copies(pieces, slots, table, sems, buf, device, lowest, place):
    jobs = []
    for t, (number, block) in enumerate(slots):
        unit = held_unit(table[:, t], device)
        copy = pltpu.make_async_copy(
            pieces[number].at[pl.ds(block * DOC_UNIT, DOC_UNIT)],
            buf.at[rows_of(place(unit), 1)],
            sems.at[t],
        )
        jobs.append((unit >= lowest, copy))
        pl.when(unit >= lowest)(copy.start)

    def arrived():
        for wanted, copy in jobs:
            pl.when(wanted)(copy.wait)

    return arrived


def late_units(device):
    chip = device >> 1
    return 4 * chip - 3, 4 * chip - 1


def first_kernel(plan, docs_ref, q_all, *refs):
    slots, table, n_pieces, window, each, group, heads = plan
    pieces = refs[:n_pieces]
    mixed_ref, top_ref, buf, sems = refs[n_pieces:]
    device = lax.axis_index("seq")
    first_unit = device * each
    base = first_unit + each - window
    late = late_units(device)
    columns = group * HEAD_DIM

    def place(unit):
        return unit - base - (unit > late[0]).astype(jnp.int32) - (unit > late[1]).astype(jnp.int32)

    unit_copies(
        pieces, slots, table, sems, buf, device, doc_start(docs_ref, first_unit), place
    )()
    steps = heads // FIRST_HEADS * each

    def one_step(step, carry):
        first_head, part = lax.div(step, each) * FIRST_HEADS, lax.rem(step, each)
        unit = first_unit + part
        start = doc_start(docs_ref, unit)
        skipped = sum(((u >= start) & (u <= unit)).astype(jnp.int32) for u in late)
        here = unit - start + 1 - skipped
        for units in range(1, window - each):

            @pl.when(here == units)
            def _():
                rows = rows_of(place(unit) - units + 1, units)
                jobs = [(h, g) for h in range(FIRST_HEADS) for g in range(0, group, CHUNK)]

                def begin(job):
                    head, g = first_head + job[0], job[1]
                    q = q_all[rows_of(part, 1), columns_of(head, columns)]
                    keys = buf[rows, columns_of(head)]
                    return scores_of(stacked(q, range(g, g + CHUNK)), keys)

                def end(job, scores):
                    h, g = job
                    head = first_head + h
                    scores = masked_last(scores, units)
                    top = jnp.max(scores, axis=1, keepdims=True)
                    weights = jnp.exp2((scores - top) * FACTOR)
                    mine = pl.ds(g * DOC_UNIT, CHUNK * DOC_UNIT)
                    mixed_ref[head, part, mine] = mixed(weights, buf[rows, columns_of(heads + head)])
                    top_ref[head, part, mine] = jnp.broadcast_to(top, (CHUNK * DOC_UNIT, HEAD_DIM))

                in_turn(jobs, begin, end)

        return carry

    lax.fori_loop(0, steps, one_step, 0)


def last_kernel(plan, docs_ref, q_all, mixed_ref, top_ref, *refs):
    slots, table, n_pieces, _, each, group, heads = plan
    pieces = refs[:n_pieces]
    out_hbm, buf, out_all, sems, out_sems = refs[n_pieces:]
    device = lax.axis_index("seq")
    first_unit = device * each
    late = late_units(device)
    columns = group * HEAD_DIM
    steps = heads // LAST_HEADS * each
    place = lambda unit: (unit > late[0]).astype(jnp.int32)
    unit_copies(pieces, slots, table, sems, buf, device, 0, place)()

    def copy_out(part):
        there = rows_of(part, 1)
        return pltpu.make_async_copy(out_all.at[there], out_hbm.at[there], out_sems.at[part])

    def one_step(step, carry):
        part, first_head = lax.rem(step, each), lax.div(step, each) * LAST_HEADS
        unit = first_unit + part
        start = doc_start(docs_ref, unit)
        count = sum((u >= start).astype(jnp.int32) for u in late)
        jobs = [(h, g) for h in range(LAST_HEADS) for g in range(0, group, CHUNK)]

        def older(ref, job):
            return ref[first_head + job[0], part, pl.ds(job[1] * DOC_UNIT, CHUNK * DOC_UNIT)]

        def mean(result):
            return result[:, :HEAD_DIM] / result[:, HEAD_DIM:]

        def store(job, rows):
            for k in range(CHUNK):
                head = (first_head + job[0]) * group + job[1] + k
                out_all[rows_of(part, 1), columns_of(head)] = rows[
                    k * DOC_UNIT : (k + 1) * DOC_UNIT
                ].astype(out_all.dtype)

        @pl.when(count == 0)
        def _():
            for job in jobs:
                store(job, mean(older(mixed_ref, job)))

        @pl.when(count > 0)
        def _():
            def begin(job):
                head = first_head + job[0]
                q = q_all[rows_of(part, 1), columns_of(head, columns)]
                return scores_of(stacked(q, range(job[1], job[1] + CHUNK)), buf[:, columns_of(head)])

            def end(job, scores):
                head = first_head + job[0]
                column = lax.broadcasted_iota(jnp.int32, scores.shape, 1)
                scores = jnp.where(column >= (2 - count) * DOC_UNIT, scores, -jnp.inf)
                old = older(top_ref, job)
                top = jnp.maximum(old, jnp.max(scores, axis=1, keepdims=True))
                weights = jnp.exp2((scores - twice(top)) * FACTOR)
                shrink = jnp.exp2((old - top) * FACTOR)
                result = mixed(weights, buf[:, columns_of(heads + head)])
                store(job, mean(older(mixed_ref, job) * twice(shrink) + result))

            in_turn(jobs, begin, end)

        @pl.when(first_head == heads - LAST_HEADS)
        def _():
            copy_out(part).start()

        return carry

    lax.fori_loop(0, steps, one_step, 0)
    for part in range(each):
        copy_out(part).wait()


def in_two(queries, doc_lengths, first, last, window, each, group, heads):
    rows = each * DOC_UNIT
    dtype = queries.dtype
    anywhere = pl.BlockSpec(memory_space=pl.ANY)
    dma = pltpu.SemaphoreType.DMA
    tile = (heads, each, group * DOC_UNIT, HEAD_DIM)
    state = (
        pltpu.VMEM((*tile[:-1], 2 * HEAD_DIM), jnp.float32),
        pltpu.VMEM(tile, jnp.float32),
    )
    on_chip = pl.BlockSpec(memory_space=pltpu.VMEM)
    is_late = lambda device, unit: unit in late_units(device)

    def call(kernel, pieces, wanted, held_rows, operands, in_specs, shapes, out_specs, scratch):
        slots, table = slots_of(pieces, window, each, wanted)
        plan = (slots, table, len(pieces), window, each, group, heads)
        scratch = [
            pltpu.VMEM((held_rows, 2 * heads * HEAD_DIM), dtype),
            *scratch(len(slots)),
        ]
        work = held_rows * rows * heads * group * HEAD_DIM * 2
        return pl.pallas_call(
            functools.partial(kernel, plan),
            out_shape=shapes,
            grid_spec=pltpu.PrefetchScalarGridSpec(
                num_scalar_prefetch=1,
                grid=(),
                in_specs=[*in_specs, *[anywhere] * len(pieces)],
                out_specs=out_specs,
                scratch_shapes=scratch,
            ),
            compiler_params=pltpu.CompilerParams(vmem_limit_bytes=VMEM_LIMIT),
            cost_estimate=pl.CostEstimate(
                flops=work, transcendentals=work // (4 * HEAD_DIM), bytes_accessed=4 * queries.size * 2
            ),
        )(doc_lengths, *operands, *[p.array for p in pieces])

    so_far = call(
        first_kernel,
        first,
        lambda device, unit: not is_late(device, unit),
        (window - 2) * DOC_UNIT,
        (queries,),
        (on_chip,),
        state,
        (on_chip, on_chip),
        lambda n: [dma((n,))],
    )
    return call(
        last_kernel,
        last,
        is_late,
        2 * DOC_UNIT,
        (queries, *so_far),
        (on_chip, on_chip, on_chip),
        jax.ShapeDtypeStruct(queries.shape, dtype),
        anywhere,
        lambda n: [pltpu.VMEM(queries.shape, dtype), dma((n,)), dma((each,))],
    )


VMEM_LIMIT = 24 << 20


def attend_kernel(plan, docs_ref, q_hbm, *refs):
    slots, table, n_pieces, window, each, group, first_head, heads, n_docs = plan
    pieces, out_hbm = refs[:n_pieces], refs[-9]
    q_all, out_all, buf, sems, q_sems, out_sems, state_m, state_o = refs[-8:]
    device = lax.axis_index("seq")
    first_unit = device * each
    base = first_unit + each - window
    width = heads * HEAD_DIM
    columns = group * HEAD_DIM

    def doc_start(unit):
        start, passed = jnp.int32(0), jnp.int32(0)
        for d in range(n_docs):
            passed = passed + docs_ref[d]
            start = jnp.where(passed <= unit, passed, start)
        return start

    lowest_unit = doc_start(first_unit)

    def each_copy(act):
        for t, (number, block) in enumerate(slots):
            held = set(table[:, t].tolist()) - {-1}
            if len(held) == 1:
                unit = jnp.int32(held.pop())
            else:
                unit = jnp.int32(-1)
                for holder in np.flatnonzero(table[:, t] >= 0):
                    unit = jnp.where(device == int(holder), int(table[holder, t]), unit)

            @pl.when((unit >= lowest_unit) & (unit < first_unit + each))
            def _():
                place = pl.multiple_of((unit - base) * DOC_UNIT, DOC_UNIT)
                act(
                    pltpu.make_async_copy(
                        pieces[number].at[pl.ds(block * DOC_UNIT, DOC_UNIT)],
                        buf.at[pl.ds(place, DOC_UNIT)],
                        sems.at[t],
                    )
                )

    def q_copy(head):
        there = pl.ds(pl.multiple_of((first_head + head) * columns, columns), columns)
        return pltpu.make_async_copy(q_hbm.at[:, there], q_all.at[head], q_sems.at[head])

    def out_copy(head):
        there = pl.ds(pl.multiple_of((first_head + head) * columns, columns), columns)
        return pltpu.make_async_copy(out_all.at[head], out_hbm.at[:, there], out_sems.at[head])

    q_copy(0).start()
    each_copy(lambda copy: copy.start())
    for head in range(1, heads):
        q_copy(head).start()
    each_copy(lambda copy: copy.wait())

    factor = HEAD_DIM**-0.5 * math.log2(math.e)
    ones = jnp.ones((min(MOST_UNITS, window) * DOC_UNIT, HEAD_DIM), buf.dtype)
    most = min(MOST_UNITS, window - each + 1)
    longer = window - each + 1 > most

    def each_head(head, carry):
        q_copy(head).wait()
        key_columns = pl.ds(pl.multiple_of(head * HEAD_DIM, HEAD_DIM), HEAD_DIM)
        value_columns = pl.ds(pl.multiple_of(width + head * HEAD_DIM, HEAD_DIM), HEAD_DIM)

        def stacked(part):
            q = q_all[head, pl.ds(part * DOC_UNIT, DOC_UNIT), :]
            return jnp.concatenate(
                [q[:, g * HEAD_DIM : (g + 1) * HEAD_DIM] for g in range(group)], axis=0
            )

        def scores_of(q, first, units):
            there = pl.ds(pl.multiple_of(first * DOC_UNIT, DOC_UNIT), units * DOC_UNIT)
            return lax.dot_general(
                q, buf[there, key_columns], (((1,), (1,)), ((), ())), preferred_element_type=jnp.float32
            )

        def mixed(weights, first, units):
            there = pl.ds(pl.multiple_of(first * DOC_UNIT, DOC_UNIT), units * DOC_UNIT)
            value_rows = jnp.concatenate([buf[there, value_columns], ones[: units * DOC_UNIT]], axis=1)
            return jnp.dot(
                weights.astype(buf.dtype), value_rows, preferred_element_type=jnp.float32
            )

        def store(part, result):
            result = result[:, :HEAD_DIM] / result[:, HEAD_DIM:]
            for g in range(group):
                out_all[
                    head, pl.ds(part * DOC_UNIT, DOC_UNIT), g * HEAD_DIM : (g + 1) * HEAD_DIM
                ] = result[g * DOC_UNIT : (g + 1) * DOC_UNIT].astype(out_all.dtype)

        for part in range(each):
            unit = first_unit + part
            start = doc_start(unit)
            count = unit - start + 1
            here = lax.rem(count - 1, most) + 1
            for units in range(1, most + 1):

                @pl.when(here == units)
                def _():
                    first = unit - base - units + 1
                    scores = scores_of(stacked(part), first, units)
                    last = scores[:, (units - 1) * DOC_UNIT :]
                    row = lax.broadcasted_iota(jnp.int32, last.shape, 0) % DOC_UNIT
                    column = lax.broadcasted_iota(jnp.int32, last.shape, 1)
                    last = jnp.where(column <= row, last, -jnp.inf)
                    if units > 1:
                        before = scores[:, : (units - 1) * DOC_UNIT]
                        scores = jnp.concatenate([before, last], axis=1)
                    else:
                        scores = last
                    top = jnp.max(scores, axis=1, keepdims=True)
                    result = mixed(jnp.exp2((scores - top) * factor), first, units)
                    if longer:
                        state_m[...], state_o[...] = top, result
                    else:
                        store(part, result)

            if longer:

                def add_block(number, carry):
                    first = start - base + number * most
                    scores = scores_of(stacked(part), first, most)
                    old = state_m[...]
                    top = jnp.maximum(old, jnp.max(scores, axis=1, keepdims=True))
                    weights = jnp.exp2((scores - top) * factor)
                    shrink = jnp.exp2((old - top) * factor)
                    state_m[...] = top
                    state_o[...] = state_o[...] * shrink + mixed(weights, first, most)
                    return carry

                lax.fori_loop(0, lax.div(count - 1, most), add_block, 0)
                store(part, state_o[...])
        out_copy(head).start()
        return carry

    lax.fori_loop(0, heads, each_head, 0)
    for head in range(heads):
        out_copy(head).wait()


def attend(queries, doc_lengths, pieces, window, each, group, first_head, heads, before):
    slots, table = slots_of(pieces, window, each)
    width = heads * HEAD_DIM
    rows = each * DOC_UNIT
    columns = group * HEAD_DIM
    plan = (slots, table, len(pieces), window, each, group, first_head, heads, doc_lengths.shape[0])
    anywhere = pl.BlockSpec(memory_space=pl.ANY)
    extra = [] if before is None else [before]
    work = window * DOC_UNIT * rows * heads * group * HEAD_DIM * 2
    n_long = group * DOC_UNIT if window - each + 1 > MOST_UNITS else 8
    held = (window * DOC_UNIT * 2 * width + 2 * rows * columns * heads) * 2
    return pl.pallas_call(
        functools.partial(attend_kernel, plan),
        out_shape=jax.ShapeDtypeStruct(queries.shape, queries.dtype),
        grid_spec=pltpu.PrefetchScalarGridSpec(
            num_scalar_prefetch=1,
            grid=(),
            in_specs=[anywhere] * (1 + len(pieces) + len(extra)),
            out_specs=anywhere,
            scratch_shapes=[
                pltpu.VMEM((heads, rows, columns), queries.dtype),
                pltpu.VMEM((heads, rows, columns), queries.dtype),
                pltpu.VMEM((window * DOC_UNIT, 2 * width), queries.dtype),
                pltpu.SemaphoreType.DMA((len(slots),)),
                pltpu.SemaphoreType.DMA((heads,)),
                pltpu.SemaphoreType.DMA((heads,)),
                pltpu.VMEM((n_long, 1), jnp.float32),
                pltpu.VMEM((n_long, 2 * HEAD_DIM), jnp.float32),
            ],
        ),
        input_output_aliases={} if before is None else {2 + len(pieces): 0},
        compiler_params=pltpu.CompilerParams(vmem_limit_bytes=held + (12 << 20)),
        cost_estimate=pl.CostEstimate(
            flops=work,
            transcendentals=work // (4 * HEAD_DIM),
            bytes_accessed=2 * rows * columns * heads * 2 + window * DOC_UNIT * width * 4,
        ),
    )(doc_lengths, queries, *[p.array for p in pieces], *extra)


def on_device(queries, keys, values, doc_lengths):
    rows = queries.shape[0]
    heads = keys.shape[1] // HEAD_DIM
    group = queries.shape[1] // keys.shape[1]
    count = lax.axis_size("seq")
    each = rows // DOC_UNIT
    longest = count * each // 2
    window = longest - 1 + each
    units = np.arange(count * each).reshape(count, each)
    if is_cube(count, each):
        low, high = (
            Piece(jnp.concatenate([keys[part], values[part]], axis=1), units[:, u : u + 1])
            for u, part in enumerate((slice(0, DOC_UNIT), slice(DOC_UNIT, rows)))
        )
        first, last = cube_exchange(low, high)
        return in_two(queries, doc_lengths, first, last, window, each, group, heads)
    out = None
    parts = PARTS_OF_HEADS
    for part in range(parts):
        first, last = heads * part // parts, heads * (part + 1) // parts
        columns = slice(first * HEAD_DIM, last * HEAD_DIM)
        both = jnp.concatenate([keys[:, columns], values[:, columns]], axis=1)
        pieces = gather_exchange(Piece(both, units))
        out = attend(
            queries, doc_lengths, pieces, window, each, group, first, last - first, out
        )
    return out


def is_cube(count, each):
    return (count, each) == (8, 2)


def solution(mesh):
    rows = P(("grp", "seq"), None)
    return jax.shard_map(on_device, mesh=mesh, in_specs=(rows, rows, rows, P("grp")), out_specs=rows, check_vma=False)
```

```python
import functools
import math

import jax
import jax.numpy as jnp
import numpy as np
from jax import lax
from jax.experimental import pallas as pl
from jax.experimental.pallas import tpu as pltpu
from jax.sharding import PartitionSpec as P


HEAD_DIM = 128
DOC_UNIT = 128
MOST_UNITS = 8
PARTS_OF_HEADS = 2


class Piece:
    def __init__(self, array, units):
        self.array, self.units = array, units

    def rows(self, first, last):
        return Piece(self.array[first * DOC_UNIT : last * DOC_UNIT], self.units[:, first:last])

    def to(self, pairs):
        units = np.full_like(self.units, -1)
        for source, target in pairs:
            units[target] = self.units[source]
        return Piece(lax.ppermute(self.array, "seq", pairs), units)


def cube_exchange(low, high):
    chip = lambda c, b: 2 * c + b
    both = (0, 1)
    swap = lambda *chips: [(chip(c, b), chip(c, 1 - b)) for c in chips for b in both]
    next_chip = [(chip(c, b), chip(c + 1, b)) for c in (0, 2) for b in both]
    beside = [(chip(c, 0), chip(c, 1)) for c in range(4)]
    b_low = low.to([(chip(0, 1), chip(2, 0))])
    b_high = high.to([(chip(0, b), chip(2, b)) for b in both])
    near_low = low.to([*next_chip, (chip(1, 0), chip(2, 1))])
    near_high = high.to(next_chip)
    a_low = low.to([(chip(1, 1), chip(3, 0))])
    a_high = high.to([(chip(1, b), chip(3, b)) for b in both])
    on_low = a_low.to([(chip(3, 0), chip(2, 0))])
    on_high = a_high.to([(chip(3, b), chip(2, b)) for b in both])
    own = [low, high, low.to(beside), high.to(beside)]
    middle = [
        a_low,
        a_high,
        b_low,
        b_high,
        near_low,
        on_low,
        near_low.to([*swap(1, 3), (chip(2, 1), chip(2, 0))]),
        on_low.to([(chip(2, 0), chip(2, 1))]),
        b_high.to([(chip(2, 1), chip(2, 0))]),
        a_high.to([(chip(3, 1), chip(3, 0))]),
    ]
    last = [near_high, on_high, near_high.to(swap(1, 3)), on_high.to(swap(2))]
    return own, middle, last


def gather_exchange(own):
    count, each = own.units.shape
    everything = lax.all_gather(own.array, "seq", axis=0, tiled=True)
    return [Piece(everything, np.tile(np.arange(count * each), (count, 1)))]


def slots_of(pieces, window, each, wanted=lambda device, unit: True):
    slots, table = [], []
    count = pieces[0].units.shape[0]
    held = [set() for _ in range(count)]
    for number, piece in enumerate(pieces):
        for block in range(piece.units.shape[1]):
            column = []
            for device in range(count):
                unit = int(piece.units[device, block])
                last = each * device + each - 1
                fits = last - window < unit <= last and unit >= 0 and unit not in held[device]
                column.append(unit if fits else -1)
                if fits:
                    held[device].add(unit)
            if max(column) >= 0:
                slots.append((number, block))
                table.append(column)
    for device in range(count):
        last = each * device + each - 1
        units = range(max(0, last - window + 1), last + 1)
        assert held[device] == {unit for unit in units if wanted(device, unit)}
    return slots, np.array(table, np.int32).T


def doc_start(docs_ref, unit):
    start, passed = jnp.int32(0), jnp.int32(0)
    for d in range(docs_ref.shape[0]):
        passed = passed + docs_ref[d]
        start = jnp.where(passed <= unit, passed, start)
    return start


def held_unit(column, device):
    held = set(column.tolist()) - {-1}
    if len(held) == 1 and (column >= 0).all():
        return jnp.int32(held.pop())
    unit = jnp.int32(-1)
    for holder in np.flatnonzero(column >= 0):
        unit = jnp.where(device == int(holder), int(column[holder]), unit)
    return unit


FACTOR = HEAD_DIM**-0.5 * math.log2(math.e)


def rows_of(first, units):
    return pl.ds(pl.multiple_of(first * DOC_UNIT, DOC_UNIT), units * DOC_UNIT)


def columns_of(head, width=HEAD_DIM):
    return pl.ds(pl.multiple_of(head * width, width), width)


def stacked(q, heads):
    return jnp.concatenate([q[:, g * HEAD_DIM : (g + 1) * HEAD_DIM] for g in heads], axis=0)


def scores_of(q, key_rows):
    return lax.dot_general(
        q, key_rows, (((1,), (1,)), ((), ())), preferred_element_type=jnp.float32
    )


def mixed(weights, value_rows):
    ones = jnp.ones(value_rows.shape, value_rows.dtype)
    return jnp.dot(
        weights.astype(value_rows.dtype),
        jnp.concatenate([value_rows, ones], axis=1),
        preferred_element_type=jnp.float32,
    )


def masked_last(scores, units):
    last = scores[:, (units - 1) * DOC_UNIT :]
    row = lax.broadcasted_iota(jnp.int32, last.shape, 0) % DOC_UNIT
    column = lax.broadcasted_iota(jnp.int32, last.shape, 1)
    last = jnp.where(column <= row, last, -jnp.inf)
    if units == 1:
        return last
    return jnp.concatenate([scores[:, : (units - 1) * DOC_UNIT], last], axis=1)


def in_turn(jobs, start, finish):
    pending = start(jobs[0])
    for number, job in enumerate(jobs):
        started = pending
        if number + 1 < len(jobs):
            pending = start(jobs[number + 1])
        finish(job, started)


CHUNK = 2
FIRST_HEADS, MIDDLE_HEADS, LAST_HEADS = 4, 4, 8


def unit_copies(pieces, slots, table, sems, buf, device, lowest, place):
    jobs = []
    for t, (number, block) in enumerate(slots):
        unit = held_unit(table[:, t], device)
        copy = pltpu.make_async_copy(
            pieces[number].at[pl.ds(block * DOC_UNIT, DOC_UNIT)],
            buf.at[rows_of(place(unit), 1)],
            sems.at[t],
        )
        jobs.append((unit >= lowest, copy))
        pl.when(unit >= lowest)(copy.start)

    def arrived():
        for wanted, copy in jobs:
            pl.when(wanted)(copy.wait)

    return arrived


def late_units(device):
    chip = device >> 1
    return 4 * chip - 3, 4 * chip - 1


def first_kernel(plan, docs_ref, q_all, *refs):
    slots, table, n_pieces, _, each, group, heads = plan
    pieces = refs[:n_pieces]
    mixed_ref, top_ref, buf, sems = refs[n_pieces:]
    device = lax.axis_index("seq")
    first_unit = device * each
    chip_unit = (device >> 1) * 2 * each
    columns = group * HEAD_DIM
    place = lambda unit: unit - chip_unit
    lowest = doc_start(docs_ref, first_unit)
    unit_copies(pieces, slots, table, sems, buf, device, lowest, place)()
    steps = heads // FIRST_HEADS * each

    def one_step(step, carry):
        first_head, part = lax.div(step, each) * FIRST_HEADS, lax.rem(step, each)
        unit = first_unit + part
        here = unit - jnp.maximum(doc_start(docs_ref, unit), chip_unit) + 1
        for units in range(1, 2 * each + 1):

            @pl.when(here == units)
            def _():
                rows = rows_of(place(unit) - units + 1, units)
                jobs = [(h, g) for h in range(FIRST_HEADS) for g in range(0, group, CHUNK)]

                def begin(job):
                    head, g = first_head + job[0], job[1]
                    q = q_all[rows_of(part, 1), columns_of(head, columns)]
                    keys = buf[rows, columns_of(head)]
                    return scores_of(stacked(q, range(g, g + CHUNK)), keys)

                def end(job, scores):
                    h, g = job
                    head = first_head + h
                    scores = masked_last(scores, units)
                    top = jnp.max(scores, axis=1, keepdims=True)
                    weights = jnp.exp2((scores - top) * FACTOR)
                    mine = pl.ds(g * DOC_UNIT, CHUNK * DOC_UNIT)
                    mixed_ref[head, part, mine] = mixed(weights, buf[rows, columns_of(heads + head)])
                    top_ref[head, part, mine] = jnp.broadcast_to(top, (CHUNK * DOC_UNIT, HEAD_DIM))

                in_turn(jobs, begin, end)

        return carry

    lax.fori_loop(0, steps, one_step, 0)


def add_rows(old_mixed, old_top, scores, value_rows):
    top = jnp.maximum(old_top, jnp.max(scores, axis=1, keepdims=True))
    wide = jnp.concatenate([top] * (scores.shape[1] // HEAD_DIM), axis=1)
    weights = jnp.exp2((scores - wide) * FACTOR)
    shrink = jnp.exp2((old_top - top) * FACTOR)
    both = jnp.concatenate([shrink, shrink], axis=1)
    return old_mixed * both + mixed(weights, value_rows), top


def middle_kernel(plan, docs_ref, q_all, old_mixed, old_top, *refs):
    slots, table, n_pieces, window, each, group, heads = plan
    pieces = refs[:n_pieces]
    mixed_ref, top_ref, buf, sems = refs[n_pieces:]
    device = lax.axis_index("seq")
    first_unit = device * each
    chip_unit = (device >> 1) * 2 * each
    late = late_units(device)
    columns = group * HEAD_DIM
    most = window - each - 2
    steps = heads // MIDDLE_HEADS * each
    place = lambda unit: unit - (chip_unit - most - 2) - (unit > late[0]).astype(jnp.int32)
    lowest = doc_start(docs_ref, first_unit)
    unit_copies(pieces, slots, table, sems, buf, device, lowest, place)()

    def one_step(step, carry):
        first_head, part = lax.div(step, each) * MIDDLE_HEADS, lax.rem(step, each)
        start = doc_start(docs_ref, first_unit + part)
        here = chip_unit - start - sum((u >= start).astype(jnp.int32) for u in late)
        for units in range(1, most + 1):

            @pl.when(here == units)
            def _():
                rows = pl.ds((most - units) * DOC_UNIT, units * DOC_UNIT)
                jobs = [(h, g) for h in range(MIDDLE_HEADS) for g in range(0, group, CHUNK)]

                def begin(job):
                    head, g = first_head + job[0], job[1]
                    q = q_all[rows_of(part, 1), columns_of(head, columns)]
                    return scores_of(stacked(q, range(g, g + CHUNK)), buf[rows, columns_of(head)])

                def end(job, scores):
                    head = first_head + job[0]
                    at = (head, part, pl.ds(job[1] * DOC_UNIT, CHUNK * DOC_UNIT))
                    mixed_ref[at], top_ref[at] = add_rows(
                        old_mixed[at], old_top[at], scores, buf[rows, columns_of(heads + head)]
                    )

                in_turn(jobs, begin, end)

        return carry

    lax.fori_loop(0, steps, one_step, 0)


def last_kernel(plan, docs_ref, q_all, mixed_ref, top_ref, *refs):
    slots, table, n_pieces, _, each, group, heads = plan
    pieces = refs[:n_pieces]
    out_hbm, buf, out_all, sems, out_sems = refs[n_pieces:]
    device = lax.axis_index("seq")
    first_unit = device * each
    late = late_units(device)
    columns = group * HEAD_DIM
    steps = heads // LAST_HEADS * each
    place = lambda unit: (unit > late[0]).astype(jnp.int32)
    unit_copies(pieces, slots, table, sems, buf, device, 0, place)()

    def copy_out(part):
        there = rows_of(part, 1)
        return pltpu.make_async_copy(out_all.at[there], out_hbm.at[there], out_sems.at[part])

    def one_step(step, carry):
        part, first_head = lax.rem(step, each), lax.div(step, each) * LAST_HEADS
        unit = first_unit + part
        start = doc_start(docs_ref, unit)
        count = sum((u >= start).astype(jnp.int32) for u in late)
        jobs = [(h, g) for h in range(LAST_HEADS) for g in range(0, group, CHUNK)]

        def older(ref, job):
            return ref[first_head + job[0], part, pl.ds(job[1] * DOC_UNIT, CHUNK * DOC_UNIT)]

        def mean(result):
            return result[:, :HEAD_DIM] / result[:, HEAD_DIM:]

        def store(job, rows):
            for k in range(CHUNK):
                head = (first_head + job[0]) * group + job[1] + k
                out_all[rows_of(part, 1), columns_of(head)] = rows[
                    k * DOC_UNIT : (k + 1) * DOC_UNIT
                ].astype(out_all.dtype)

        @pl.when(count == 0)
        def _():
            for job in jobs:
                store(job, mean(older(mixed_ref, job)))

        @pl.when(count > 0)
        def _():
            def begin(job):
                head = first_head + job[0]
                q = q_all[rows_of(part, 1), columns_of(head, columns)]
                return scores_of(stacked(q, range(job[1], job[1] + CHUNK)), buf[:, columns_of(head)])

            def end(job, scores):
                head = first_head + job[0]
                column = lax.broadcasted_iota(jnp.int32, scores.shape, 1)
                scores = jnp.where(column >= (2 - count) * DOC_UNIT, scores, -jnp.inf)
                result, _ = add_rows(
                    older(mixed_ref, job), older(top_ref, job), scores, buf[:, columns_of(heads + head)]
                )
                store(job, mean(result))

            in_turn(jobs, begin, end)

        @pl.when(first_head == heads - LAST_HEADS)
        def _():
            copy_out(part).start()

        return carry

    lax.fori_loop(0, steps, one_step, 0)
    for part in range(each):
        copy_out(part).wait()


def in_stages(queries, doc_lengths, first, middle, last, window, each, group, heads):
    rows = each * DOC_UNIT
    dtype = queries.dtype
    anywhere = pl.BlockSpec(memory_space=pl.ANY)
    dma = pltpu.SemaphoreType.DMA
    tile = (heads, each, group * DOC_UNIT, HEAD_DIM)
    state = (
        pltpu.VMEM((*tile[:-1], 2 * HEAD_DIM), jnp.float32),
        pltpu.VMEM(tile, jnp.float32),
    )
    on_chip = pl.BlockSpec(memory_space=pltpu.VMEM)
    is_late = lambda device, unit: unit in late_units(device)
    is_own = lambda device, unit: unit >= (device >> 1) * 2 * each

    def call(kernel, pieces, wanted, held_rows, operands, in_specs, shapes, out_specs, scratch, aliases={}):
        slots, table = slots_of(pieces, window, each, wanted)
        plan = (slots, table, len(pieces), window, each, group, heads)
        scratch = [
            pltpu.VMEM((held_rows, 2 * heads * HEAD_DIM), dtype),
            *scratch(len(slots)),
        ]
        work = held_rows * rows * heads * group * HEAD_DIM * 2
        return pl.pallas_call(
            functools.partial(kernel, plan),
            out_shape=shapes,
            grid_spec=pltpu.PrefetchScalarGridSpec(
                num_scalar_prefetch=1,
                grid=(),
                in_specs=[*in_specs, *[anywhere] * len(pieces)],
                out_specs=out_specs,
                scratch_shapes=scratch,
            ),
            input_output_aliases=aliases,
            compiler_params=pltpu.CompilerParams(vmem_limit_bytes=VMEM_LIMIT),
            cost_estimate=pl.CostEstimate(
                flops=work, transcendentals=work // (4 * HEAD_DIM), bytes_accessed=4 * queries.size * 2
            ),
        )(doc_lengths, *operands, *[p.array for p in pieces])

    so_far = call(
        first_kernel,
        first,
        is_own,
        2 * each * DOC_UNIT,
        (queries,),
        (on_chip,),
        state,
        (on_chip, on_chip),
        lambda n: [dma((n,))],
    )
    so_far = call(
        middle_kernel,
        middle,
        lambda device, unit: not is_own(device, unit) and not is_late(device, unit),
        (window - each - 2) * DOC_UNIT,
        (queries, *so_far),
        (on_chip, on_chip, on_chip),
        state,
        (on_chip, on_chip),
        lambda n: [dma((n,))],
        {2: 0, 3: 1},
    )
    return call(
        last_kernel,
        last,
        is_late,
        2 * DOC_UNIT,
        (queries, *so_far),
        (on_chip, on_chip, on_chip),
        jax.ShapeDtypeStruct(queries.shape, dtype),
        anywhere,
        lambda n: [pltpu.VMEM(queries.shape, dtype), dma((n,)), dma((each,))],
    )


VMEM_LIMIT = 24 << 20


def attend_kernel(plan, docs_ref, q_hbm, *refs):
    slots, table, n_pieces, window, each, group, first_head, heads, n_docs = plan
    pieces, out_hbm = refs[:n_pieces], refs[-9]
    q_all, out_all, buf, sems, q_sems, out_sems, state_m, state_o = refs[-8:]
    device = lax.axis_index("seq")
    first_unit = device * each
    base = first_unit + each - window
    width = heads * HEAD_DIM
    columns = group * HEAD_DIM

    def doc_start(unit):
        start, passed = jnp.int32(0), jnp.int32(0)
        for d in range(n_docs):
            passed = passed + docs_ref[d]
            start = jnp.where(passed <= unit, passed, start)
        return start

    lowest_unit = doc_start(first_unit)

    def each_copy(act):
        for t, (number, block) in enumerate(slots):
            held = set(table[:, t].tolist()) - {-1}
            if len(held) == 1:
                unit = jnp.int32(held.pop())
            else:
                unit = jnp.int32(-1)
                for holder in np.flatnonzero(table[:, t] >= 0):
                    unit = jnp.where(device == int(holder), int(table[holder, t]), unit)

            @pl.when((unit >= lowest_unit) & (unit < first_unit + each))
            def _():
                place = pl.multiple_of((unit - base) * DOC_UNIT, DOC_UNIT)
                act(
                    pltpu.make_async_copy(
                        pieces[number].at[pl.ds(block * DOC_UNIT, DOC_UNIT)],
                        buf.at[pl.ds(place, DOC_UNIT)],
                        sems.at[t],
                    )
                )

    def q_copy(head):
        there = pl.ds(pl.multiple_of((first_head + head) * columns, columns), columns)
        return pltpu.make_async_copy(q_hbm.at[:, there], q_all.at[head], q_sems.at[head])

    def out_copy(head):
        there = pl.ds(pl.multiple_of((first_head + head) * columns, columns), columns)
        return pltpu.make_async_copy(out_all.at[head], out_hbm.at[:, there], out_sems.at[head])

    q_copy(0).start()
    each_copy(lambda copy: copy.start())
    for head in range(1, heads):
        q_copy(head).start()
    each_copy(lambda copy: copy.wait())

    factor = HEAD_DIM**-0.5 * math.log2(math.e)
    ones = jnp.ones((min(MOST_UNITS, window) * DOC_UNIT, HEAD_DIM), buf.dtype)
    most = min(MOST_UNITS, window - each + 1)
    longer = window - each + 1 > most

    def each_head(head, carry):
        q_copy(head).wait()
        key_columns = pl.ds(pl.multiple_of(head * HEAD_DIM, HEAD_DIM), HEAD_DIM)
        value_columns = pl.ds(pl.multiple_of(width + head * HEAD_DIM, HEAD_DIM), HEAD_DIM)

        def stacked(part):
            q = q_all[head, pl.ds(part * DOC_UNIT, DOC_UNIT), :]
            return jnp.concatenate(
                [q[:, g * HEAD_DIM : (g + 1) * HEAD_DIM] for g in range(group)], axis=0
            )

        def scores_of(q, first, units):
            there = pl.ds(pl.multiple_of(first * DOC_UNIT, DOC_UNIT), units * DOC_UNIT)
            return lax.dot_general(
                q, buf[there, key_columns], (((1,), (1,)), ((), ())), preferred_element_type=jnp.float32
            )

        def mixed(weights, first, units):
            there = pl.ds(pl.multiple_of(first * DOC_UNIT, DOC_UNIT), units * DOC_UNIT)
            value_rows = jnp.concatenate([buf[there, value_columns], ones[: units * DOC_UNIT]], axis=1)
            return jnp.dot(
                weights.astype(buf.dtype), value_rows, preferred_element_type=jnp.float32
            )

        def store(part, result):
            result = result[:, :HEAD_DIM] / result[:, HEAD_DIM:]
            for g in range(group):
                out_all[
                    head, pl.ds(part * DOC_UNIT, DOC_UNIT), g * HEAD_DIM : (g + 1) * HEAD_DIM
                ] = result[g * DOC_UNIT : (g + 1) * DOC_UNIT].astype(out_all.dtype)

        for part in range(each):
            unit = first_unit + part
            start = doc_start(unit)
            count = unit - start + 1
            here = lax.rem(count - 1, most) + 1
            for units in range(1, most + 1):

                @pl.when(here == units)
                def _():
                    first = unit - base - units + 1
                    scores = scores_of(stacked(part), first, units)
                    last = scores[:, (units - 1) * DOC_UNIT :]
                    row = lax.broadcasted_iota(jnp.int32, last.shape, 0) % DOC_UNIT
                    column = lax.broadcasted_iota(jnp.int32, last.shape, 1)
                    last = jnp.where(column <= row, last, -jnp.inf)
                    if units > 1:
                        before = scores[:, : (units - 1) * DOC_UNIT]
                        scores = jnp.concatenate([before, last], axis=1)
                    else:
                        scores = last
                    top = jnp.max(scores, axis=1, keepdims=True)
                    result = mixed(jnp.exp2((scores - top) * factor), first, units)
                    if longer:
                        state_m[...], state_o[...] = top, result
                    else:
                        store(part, result)

            if longer:

                def add_block(number, carry):
                    first = start - base + number * most
                    scores = scores_of(stacked(part), first, most)
                    old = state_m[...]
                    top = jnp.maximum(old, jnp.max(scores, axis=1, keepdims=True))
                    weights = jnp.exp2((scores - top) * factor)
                    shrink = jnp.exp2((old - top) * factor)
                    state_m[...] = top
                    state_o[...] = state_o[...] * shrink + mixed(weights, first, most)
                    return carry

                lax.fori_loop(0, lax.div(count - 1, most), add_block, 0)
                store(part, state_o[...])
        out_copy(head).start()
        return carry

    lax.fori_loop(0, heads, each_head, 0)
    for head in range(heads):
        out_copy(head).wait()


def attend(queries, doc_lengths, pieces, window, each, group, first_head, heads, before):
    slots, table = slots_of(pieces, window, each)
    width = heads * HEAD_DIM
    rows = each * DOC_UNIT
    columns = group * HEAD_DIM
    plan = (slots, table, len(pieces), window, each, group, first_head, heads, doc_lengths.shape[0])
    anywhere = pl.BlockSpec(memory_space=pl.ANY)
    extra = [] if before is None else [before]
    work = window * DOC_UNIT * rows * heads * group * HEAD_DIM * 2
    n_long = group * DOC_UNIT if window - each + 1 > MOST_UNITS else 8
    held = (window * DOC_UNIT * 2 * width + 2 * rows * columns * heads) * 2
    return pl.pallas_call(
        functools.partial(attend_kernel, plan),
        out_shape=jax.ShapeDtypeStruct(queries.shape, queries.dtype),
        grid_spec=pltpu.PrefetchScalarGridSpec(
            num_scalar_prefetch=1,
            grid=(),
            in_specs=[anywhere] * (1 + len(pieces) + len(extra)),
            out_specs=anywhere,
            scratch_shapes=[
                pltpu.VMEM((heads, rows, columns), queries.dtype),
                pltpu.VMEM((heads, rows, columns), queries.dtype),
                pltpu.VMEM((window * DOC_UNIT, 2 * width), queries.dtype),
                pltpu.SemaphoreType.DMA((len(slots),)),
                pltpu.SemaphoreType.DMA((heads,)),
                pltpu.SemaphoreType.DMA((heads,)),
                pltpu.VMEM((n_long, 1), jnp.float32),
                pltpu.VMEM((n_long, 2 * HEAD_DIM), jnp.float32),
            ],
        ),
        input_output_aliases={} if before is None else {2 + len(pieces): 0},
        compiler_params=pltpu.CompilerParams(vmem_limit_bytes=held + (12 << 20)),
        cost_estimate=pl.CostEstimate(
            flops=work,
            transcendentals=work // (4 * HEAD_DIM),
            bytes_accessed=2 * rows * columns * heads * 2 + window * DOC_UNIT * width * 4,
        ),
    )(doc_lengths, queries, *[p.array for p in pieces], *extra)


def on_device(queries, keys, values, doc_lengths):
    rows = queries.shape[0]
    heads = keys.shape[1] // HEAD_DIM
    group = queries.shape[1] // keys.shape[1]
    count = lax.axis_size("seq")
    each = rows // DOC_UNIT
    longest = count * each // 2
    window = longest - 1 + each
    units = np.arange(count * each).reshape(count, each)
    if is_cube(count, each):
        low, high = (
            Piece(jnp.concatenate([keys[part], values[part]], axis=1), units[:, u : u + 1])
            for u, part in enumerate((slice(0, DOC_UNIT), slice(DOC_UNIT, rows)))
        )
        pieces = cube_exchange(low, high)
        return in_stages(queries, doc_lengths, *pieces, window, each, group, heads)
    out = None
    parts = PARTS_OF_HEADS
    for part in range(parts):
        first, last = heads * part // parts, heads * (part + 1) // parts
        columns = slice(first * HEAD_DIM, last * HEAD_DIM)
        both = jnp.concatenate([keys[:, columns], values[:, columns]], axis=1)
        pieces = gather_exchange(Piece(both, units))
        out = attend(
            queries, doc_lengths, pieces, window, each, group, first, last - first, out
        )
    return out


def is_cube(count, each):
    return (count, each) == (8, 2)


def solution(mesh):
    rows = P(("grp", "seq"), None)
    return jax.shard_map(on_device, mesh=mesh, in_specs=(rows, rows, rows, P("grp")), out_specs=rows, check_vma=False)
```

```python
import functools
import math

import jax
import jax.numpy as jnp
import numpy as np
from jax import lax
from jax.experimental import pallas as pl
from jax.experimental.pallas import tpu as pltpu
from jax.sharding import PartitionSpec as P


HEAD_DIM = 128
DOC_UNIT = 128
MOST_UNITS = 8
PARTS_OF_HEADS = 2


class Piece:
    def __init__(self, array, units):
        self.array, self.units = array, units

    def rows(self, first, last):
        return Piece(self.array[first * DOC_UNIT : last * DOC_UNIT], self.units[:, first:last])

    def to(self, pairs):
        units = np.full_like(self.units, -1)
        for source, target in pairs:
            units[target] = self.units[source]
        return Piece(lax.ppermute(self.array, "seq", pairs), units)


def cube_exchange(low, high):
    chip = lambda c, b: 2 * c + b
    both = (0, 1)
    swap = lambda *chips: [(chip(c, b), chip(c, 1 - b)) for c in chips for b in both]
    next_chip = [(chip(c, b), chip(c + 1, b)) for c in (0, 2) for b in both]
    beside = [(chip(c, 0), chip(c, 1)) for c in range(4)]
    b_low = low.to([(chip(0, 1), chip(2, 0))])
    b_high = high.to([(chip(0, b), chip(2, b)) for b in both])
    near_low = low.to([*next_chip, (chip(1, 0), chip(2, 1))])
    near_high = high.to(next_chip)
    a_low = low.to([(chip(1, 1), chip(3, 0))])
    a_high = high.to([(chip(1, b), chip(3, b)) for b in both])
    on_low = a_low.to([(chip(3, 0), chip(2, 0))])
    on_high = a_high.to([(chip(3, b), chip(2, b)) for b in both])
    own = [low, high, low.to(beside), high.to(beside)]
    middle = [
        a_low,
        a_high,
        b_low,
        b_high,
        near_low,
        on_low,
        near_low.to([*swap(1, 3), (chip(2, 1), chip(2, 0))]),
        on_low.to([(chip(2, 0), chip(2, 1))]),
        b_high.to([(chip(2, 1), chip(2, 0))]),
        a_high.to([(chip(3, 1), chip(3, 0))]),
    ]
    last = [near_high, on_high, near_high.to(swap(1, 3)), on_high.to(swap(2))]
    return own, middle, last


def gather_exchange(own):
    count, each = own.units.shape
    everything = lax.all_gather(own.array, "seq", axis=0, tiled=True)
    return [Piece(everything, np.tile(np.arange(count * each), (count, 1)))]


def slots_of(pieces, window, each, wanted=lambda device, unit: True):
    slots, table = [], []
    count = pieces[0].units.shape[0]
    held = [set() for _ in range(count)]
    for number, piece in enumerate(pieces):
        for block in range(piece.units.shape[1]):
            column = []
            for device in range(count):
                unit = int(piece.units[device, block])
                last = each * device + each - 1
                fits = last - window < unit <= last and unit >= 0 and unit not in held[device]
                column.append(unit if fits else -1)
                if fits:
                    held[device].add(unit)
            if max(column) >= 0:
                slots.append((number, block))
                table.append(column)
    for device in range(count):
        last = each * device + each - 1
        units = range(max(0, last - window + 1), last + 1)
        assert held[device] == {unit for unit in units if wanted(device, unit)}
    return slots, np.array(table, np.int32).T


def doc_start(docs_ref, unit):
    start, passed = jnp.int32(0), jnp.int32(0)
    for d in range(docs_ref.shape[0]):
        passed = passed + docs_ref[d]
        start = jnp.where(passed <= unit, passed, start)
    return start


def held_unit(column, device):
    held = set(column.tolist()) - {-1}
    if len(held) == 1 and (column >= 0).all():
        return jnp.int32(held.pop())
    unit = jnp.int32(-1)
    for holder in np.flatnonzero(column >= 0):
        unit = jnp.where(device == int(holder), int(column[holder]), unit)
    return unit


FACTOR = HEAD_DIM**-0.5 * math.log2(math.e)


def rows_of(first, units):
    return pl.ds(pl.multiple_of(first * DOC_UNIT, DOC_UNIT), units * DOC_UNIT)


def columns_of(head, width=HEAD_DIM):
    return pl.ds(pl.multiple_of(head * width, width), width)


def stacked(q, heads):
    return jnp.concatenate([q[:, g * HEAD_DIM : (g + 1) * HEAD_DIM] for g in heads], axis=0)


def scores_of(q, key_rows):
    return lax.dot_general(
        q, key_rows, (((1,), (1,)), ((), ())), preferred_element_type=jnp.float32
    )


def mixed(weights, value_rows):
    ones = jnp.ones(value_rows.shape, value_rows.dtype)
    return jnp.dot(
        weights.astype(value_rows.dtype),
        jnp.concatenate([value_rows, ones], axis=1),
        preferred_element_type=jnp.float32,
    )


def masked_last(scores, units):
    last = scores[:, (units - 1) * DOC_UNIT :]
    row = lax.broadcasted_iota(jnp.int32, last.shape, 0) % DOC_UNIT
    column = lax.broadcasted_iota(jnp.int32, last.shape, 1)
    last = jnp.where(column <= row, last, -jnp.inf)
    if units == 1:
        return last
    return jnp.concatenate([scores[:, : (units - 1) * DOC_UNIT], last], axis=1)


def in_turn(jobs, start, finish):
    pending = start(jobs[0])
    for number, job in enumerate(jobs):
        started = pending
        if number + 1 < len(jobs):
            pending = start(jobs[number + 1])
        finish(job, started)


CHUNK = 4
FIRST_HEADS, MIDDLE_HEADS, LAST_HEADS = 4, 4, 8


def unit_copies(pieces, slots, table, sems, buf, device, lowest, place):
    jobs = []
    for t, (number, block) in enumerate(slots):
        unit = held_unit(table[:, t], device)
        copy = pltpu.make_async_copy(
            pieces[number].at[pl.ds(block * DOC_UNIT, DOC_UNIT)],
            buf.at[rows_of(place(unit), 1)],
            sems.at[t],
        )
        jobs.append((unit >= lowest, copy))
        pl.when(unit >= lowest)(copy.start)

    def arrived():
        for wanted, copy in jobs:
            pl.when(wanted)(copy.wait)

    return arrived


def late_units(device):
    chip = device >> 1
    return 4 * chip - 3, 4 * chip - 1


def first_kernel(plan, docs_ref, q_all, *refs):
    slots, table, n_pieces, _, each, group, heads = plan
    pieces = refs[:n_pieces]
    mixed_ref, top_ref, buf, sems = refs[n_pieces:]
    device = lax.axis_index("seq")
    first_unit = device * each
    chip_unit = (device >> 1) * 2 * each
    columns = group * HEAD_DIM
    place = lambda unit: unit - chip_unit
    lowest = doc_start(docs_ref, first_unit)
    unit_copies(pieces, slots, table, sems, buf, device, lowest, place)()
    steps = heads // FIRST_HEADS * each

    def one_step(step, carry):
        first_head, part = lax.div(step, each) * FIRST_HEADS, lax.rem(step, each)
        unit = first_unit + part
        here = unit - jnp.maximum(doc_start(docs_ref, unit), chip_unit) + 1
        for units in range(1, 2 * each + 1):

            @pl.when(here == units)
            def _():
                rows = rows_of(place(unit) - units + 1, units)
                jobs = [(h, g) for h in range(FIRST_HEADS) for g in range(0, group, CHUNK)]

                def begin(job):
                    head, g = first_head + job[0], job[1]
                    q = q_all[rows_of(part, 1), columns_of(head, columns)]
                    keys = buf[rows, columns_of(head)]
                    return scores_of(stacked(q, range(g, g + CHUNK)), keys)

                def end(job, scores):
                    h, g = job
                    head = first_head + h
                    scores = masked_last(scores, units)
                    top = jnp.max(scores, axis=1, keepdims=True)
                    weights = jnp.exp2((scores - top) * FACTOR)
                    mine = pl.ds(g * DOC_UNIT, CHUNK * DOC_UNIT)
                    mixed_ref[head, part, mine] = mixed(weights, buf[rows, columns_of(heads + head)])
                    top_ref[head, part, mine] = jnp.broadcast_to(top, (CHUNK * DOC_UNIT, HEAD_DIM))

                in_turn(jobs, begin, end)

        return carry

    lax.fori_loop(0, steps, one_step, 0)


def add_rows(old_mixed, old_top, scores, value_rows):
    top = jnp.maximum(old_top, jnp.max(scores, axis=1, keepdims=True))
    wide = jnp.concatenate([top] * (scores.shape[1] // HEAD_DIM), axis=1)
    weights = jnp.exp2((scores - wide) * FACTOR)
    shrink = jnp.exp2((old_top - top) * FACTOR)
    both = jnp.concatenate([shrink, shrink], axis=1)
    return old_mixed * both + mixed(weights, value_rows), top


def middle_kernel(plan, docs_ref, q_all, old_mixed, old_top, *refs):
    slots, table, n_pieces, window, each, group, heads = plan
    pieces = refs[:n_pieces]
    mixed_ref, top_ref, buf, sems = refs[n_pieces:]
    device = lax.axis_index("seq")
    first_unit = device * each
    chip_unit = (device >> 1) * 2 * each
    late = late_units(device)
    columns = group * HEAD_DIM
    most = window - each - 2
    steps = heads // MIDDLE_HEADS * each
    place = lambda unit: unit - (chip_unit - most - 2) - (unit > late[0]).astype(jnp.int32)
    lowest = doc_start(docs_ref, first_unit)
    unit_copies(pieces, slots, table, sems, buf, device, lowest, place)()

    def one_step(step, carry):
        first_head, part = lax.div(step, each) * MIDDLE_HEADS, lax.rem(step, each)
        start = doc_start(docs_ref, first_unit + part)
        here = chip_unit - start - sum((u >= start).astype(jnp.int32) for u in late)
        for units in range(1, most + 1):

            @pl.when(here == units)
            def _():
                rows = pl.ds((most - units) * DOC_UNIT, units * DOC_UNIT)
                jobs = [(h, g) for h in range(MIDDLE_HEADS) for g in range(0, group, CHUNK)]

                def begin(job):
                    head, g = first_head + job[0], job[1]
                    q = q_all[rows_of(part, 1), columns_of(head, columns)]
                    return scores_of(stacked(q, range(g, g + CHUNK)), buf[rows, columns_of(head)])

                def end(job, scores):
                    head = first_head + job[0]
                    at = (head, part, pl.ds(job[1] * DOC_UNIT, CHUNK * DOC_UNIT))
                    mixed_ref[at], top_ref[at] = add_rows(
                        old_mixed[at], old_top[at], scores, buf[rows, columns_of(heads + head)]
                    )

                in_turn(jobs, begin, end)

        return carry

    lax.fori_loop(0, steps, one_step, 0)


def last_kernel(plan, docs_ref, q_all, mixed_ref, top_ref, *refs):
    slots, table, n_pieces, _, each, group, heads = plan
    pieces = refs[:n_pieces]
    out_hbm, buf, out_all, sems, out_sems = refs[n_pieces:]
    device = lax.axis_index("seq")
    first_unit = device * each
    late = late_units(device)
    columns = group * HEAD_DIM
    steps = heads // LAST_HEADS * each
    place = lambda unit: (unit > late[0]).astype(jnp.int32)
    unit_copies(pieces, slots, table, sems, buf, device, 0, place)()

    def copy_out(step):
        part, which = lax.rem(step, each), lax.div(step, each)
        there = (rows_of(part, 1), columns_of(which, LAST_HEADS * columns))
        return pltpu.make_async_copy(out_all.at[there], out_hbm.at[there], out_sems.at[step])

    def one_step(step, carry):
        part, first_head = lax.rem(step, each), lax.div(step, each) * LAST_HEADS
        unit = first_unit + part
        start = doc_start(docs_ref, unit)
        count = sum((u >= start).astype(jnp.int32) for u in late)
        jobs = [(h, g) for h in range(LAST_HEADS) for g in range(0, group, CHUNK)]

        def older(ref, job):
            return ref[first_head + job[0], part, pl.ds(job[1] * DOC_UNIT, CHUNK * DOC_UNIT)]

        def mean(result):
            return result[:, :HEAD_DIM] / result[:, HEAD_DIM:]

        def store(job, rows):
            for k in range(CHUNK):
                head = (first_head + job[0]) * group + job[1] + k
                out_all[rows_of(part, 1), columns_of(head)] = rows[
                    k * DOC_UNIT : (k + 1) * DOC_UNIT
                ].astype(out_all.dtype)

        @pl.when(count == 0)
        def _():
            for job in jobs:
                store(job, mean(older(mixed_ref, job)))

        for units in (1, 2):

            @pl.when(count == units)
            def _():
                rows = pl.ds((2 - units) * DOC_UNIT, units * DOC_UNIT)

                def begin(job):
                    head = first_head + job[0]
                    q = q_all[rows_of(part, 1), columns_of(head, columns)]
                    heads_here = range(job[1], job[1] + CHUNK)
                    return scores_of(stacked(q, heads_here), buf[rows, columns_of(head)])

                def end(job, scores):
                    value_rows = buf[rows, columns_of(heads + first_head + job[0])]
                    state = older(mixed_ref, job), older(top_ref, job)
                    store(job, mean(add_rows(*state, scores, value_rows)[0]))

                in_turn(jobs, begin, end)

        copy_out(step).start()
        return carry

    lax.fori_loop(0, steps, one_step, 0)
    for step in range(steps):
        copy_out(step).wait()


def in_stages(queries, doc_lengths, first, middle, last, window, each, group, heads):
    rows = each * DOC_UNIT
    dtype = queries.dtype
    anywhere = pl.BlockSpec(memory_space=pl.ANY)
    dma = pltpu.SemaphoreType.DMA
    tile = (heads, each, group * DOC_UNIT, HEAD_DIM)
    state = (
        pltpu.VMEM((*tile[:-1], 2 * HEAD_DIM), jnp.float32),
        pltpu.VMEM(tile, jnp.float32),
    )
    on_chip = pl.BlockSpec(memory_space=pltpu.VMEM)
    is_late = lambda device, unit: unit in late_units(device)
    is_own = lambda device, unit: unit >= (device >> 1) * 2 * each

    def call(kernel, pieces, wanted, held_rows, operands, in_specs, shapes, out_specs, scratch, aliases={}):
        slots, table = slots_of(pieces, window, each, wanted)
        plan = (slots, table, len(pieces), window, each, group, heads)
        scratch = [
            pltpu.VMEM((held_rows, 2 * heads * HEAD_DIM), dtype),
            *scratch(len(slots)),
        ]
        work = held_rows * rows * heads * group * HEAD_DIM * 2
        return pl.pallas_call(
            functools.partial(kernel, plan),
            out_shape=shapes,
            grid_spec=pltpu.PrefetchScalarGridSpec(
                num_scalar_prefetch=1,
                grid=(),
                in_specs=[*in_specs, *[anywhere] * len(pieces)],
                out_specs=out_specs,
                scratch_shapes=scratch,
            ),
            input_output_aliases=aliases,
            compiler_params=pltpu.CompilerParams(vmem_limit_bytes=VMEM_LIMIT),
            cost_estimate=pl.CostEstimate(
                flops=work, transcendentals=work // (4 * HEAD_DIM), bytes_accessed=4 * queries.size * 2
            ),
        )(doc_lengths, *operands, *[p.array for p in pieces])

    so_far = call(
        first_kernel,
        first,
        is_own,
        2 * each * DOC_UNIT,
        (queries,),
        (on_chip,),
        state,
        (on_chip, on_chip),
        lambda n: [dma((n,))],
    )
    so_far = call(
        middle_kernel,
        middle,
        lambda device, unit: not is_own(device, unit) and not is_late(device, unit),
        (window - each - 2) * DOC_UNIT,
        (queries, *so_far),
        (on_chip, on_chip, on_chip),
        state,
        (on_chip, on_chip),
        lambda n: [dma((n,))],
        {2: 0, 3: 1},
    )
    return call(
        last_kernel,
        last,
        is_late,
        2 * DOC_UNIT,
        (queries, *so_far),
        (on_chip, on_chip, on_chip),
        jax.ShapeDtypeStruct(queries.shape, dtype),
        anywhere,
        lambda n: [pltpu.VMEM(queries.shape, dtype), dma((n,)), dma((heads // LAST_HEADS * each,))],
    )


VMEM_LIMIT = 24 << 20


def attend_kernel(plan, docs_ref, q_hbm, *refs):
    slots, table, n_pieces, window, each, group, first_head, heads, n_docs = plan
    pieces, out_hbm = refs[:n_pieces], refs[-9]
    q_all, out_all, buf, sems, q_sems, out_sems, state_m, state_o = refs[-8:]
    device = lax.axis_index("seq")
    first_unit = device * each
    base = first_unit + each - window
    width = heads * HEAD_DIM
    columns = group * HEAD_DIM

    def doc_start(unit):
        start, passed = jnp.int32(0), jnp.int32(0)
        for d in range(n_docs):
            passed = passed + docs_ref[d]
            start = jnp.where(passed <= unit, passed, start)
        return start

    lowest_unit = doc_start(first_unit)

    def each_copy(act):
        for t, (number, block) in enumerate(slots):
            held = set(table[:, t].tolist()) - {-1}
            if len(held) == 1:
                unit = jnp.int32(held.pop())
            else:
                unit = jnp.int32(-1)
                for holder in np.flatnonzero(table[:, t] >= 0):
                    unit = jnp.where(device == int(holder), int(table[holder, t]), unit)

            @pl.when((unit >= lowest_unit) & (unit < first_unit + each))
            def _():
                place = pl.multiple_of((unit - base) * DOC_UNIT, DOC_UNIT)
                act(
                    pltpu.make_async_copy(
                        pieces[number].at[pl.ds(block * DOC_UNIT, DOC_UNIT)],
                        buf.at[pl.ds(place, DOC_UNIT)],
                        sems.at[t],
                    )
                )

    def q_copy(head):
        there = pl.ds(pl.multiple_of((first_head + head) * columns, columns), columns)
        return pltpu.make_async_copy(q_hbm.at[:, there], q_all.at[head], q_sems.at[head])

    def out_copy(head):
        there = pl.ds(pl.multiple_of((first_head + head) * columns, columns), columns)
        return pltpu.make_async_copy(out_all.at[head], out_hbm.at[:, there], out_sems.at[head])

    q_copy(0).start()
    each_copy(lambda copy: copy.start())
    for head in range(1, heads):
        q_copy(head).start()
    each_copy(lambda copy: copy.wait())

    factor = HEAD_DIM**-0.5 * math.log2(math.e)
    ones = jnp.ones((min(MOST_UNITS, window) * DOC_UNIT, HEAD_DIM), buf.dtype)
    most = min(MOST_UNITS, window - each + 1)
    longer = window - each + 1 > most

    def each_head(head, carry):
        q_copy(head).wait()
        key_columns = pl.ds(pl.multiple_of(head * HEAD_DIM, HEAD_DIM), HEAD_DIM)
        value_columns = pl.ds(pl.multiple_of(width + head * HEAD_DIM, HEAD_DIM), HEAD_DIM)

        def stacked(part):
            q = q_all[head, pl.ds(part * DOC_UNIT, DOC_UNIT), :]
            return jnp.concatenate(
                [q[:, g * HEAD_DIM : (g + 1) * HEAD_DIM] for g in range(group)], axis=0
            )

        def scores_of(q, first, units):
            there = pl.ds(pl.multiple_of(first * DOC_UNIT, DOC_UNIT), units * DOC_UNIT)
            return lax.dot_general(
                q, buf[there, key_columns], (((1,), (1,)), ((), ())), preferred_element_type=jnp.float32
            )

        def mixed(weights, first, units):
            there = pl.ds(pl.multiple_of(first * DOC_UNIT, DOC_UNIT), units * DOC_UNIT)
            value_rows = jnp.concatenate([buf[there, value_columns], ones[: units * DOC_UNIT]], axis=1)
            return jnp.dot(
                weights.astype(buf.dtype), value_rows, preferred_element_type=jnp.float32
            )

        def store(part, result):
            result = result[:, :HEAD_DIM] / result[:, HEAD_DIM:]
            for g in range(group):
                out_all[
                    head, pl.ds(part * DOC_UNIT, DOC_UNIT), g * HEAD_DIM : (g + 1) * HEAD_DIM
                ] = result[g * DOC_UNIT : (g + 1) * DOC_UNIT].astype(out_all.dtype)

        for part in range(each):
            unit = first_unit + part
            start = doc_start(unit)
            count = unit - start + 1
            here = lax.rem(count - 1, most) + 1
            for units in range(1, most + 1):

                @pl.when(here == units)
                def _():
                    first = unit - base - units + 1
                    scores = scores_of(stacked(part), first, units)
                    last = scores[:, (units - 1) * DOC_UNIT :]
                    row = lax.broadcasted_iota(jnp.int32, last.shape, 0) % DOC_UNIT
                    column = lax.broadcasted_iota(jnp.int32, last.shape, 1)
                    last = jnp.where(column <= row, last, -jnp.inf)
                    if units > 1:
                        before = scores[:, : (units - 1) * DOC_UNIT]
                        scores = jnp.concatenate([before, last], axis=1)
                    else:
                        scores = last
                    top = jnp.max(scores, axis=1, keepdims=True)
                    result = mixed(jnp.exp2((scores - top) * factor), first, units)
                    if longer:
                        state_m[...], state_o[...] = top, result
                    else:
                        store(part, result)

            if longer:

                def add_block(number, carry):
                    first = start - base + number * most
                    scores = scores_of(stacked(part), first, most)
                    old = state_m[...]
                    top = jnp.maximum(old, jnp.max(scores, axis=1, keepdims=True))
                    weights = jnp.exp2((scores - top) * factor)
                    shrink = jnp.exp2((old - top) * factor)
                    state_m[...] = top
                    state_o[...] = state_o[...] * shrink + mixed(weights, first, most)
                    return carry

                lax.fori_loop(0, lax.div(count - 1, most), add_block, 0)
                store(part, state_o[...])
        out_copy(head).start()
        return carry

    lax.fori_loop(0, heads, each_head, 0)
    for head in range(heads):
        out_copy(head).wait()


def attend(queries, doc_lengths, pieces, window, each, group, first_head, heads, before):
    slots, table = slots_of(pieces, window, each)
    width = heads * HEAD_DIM
    rows = each * DOC_UNIT
    columns = group * HEAD_DIM
    plan = (slots, table, len(pieces), window, each, group, first_head, heads, doc_lengths.shape[0])
    anywhere = pl.BlockSpec(memory_space=pl.ANY)
    extra = [] if before is None else [before]
    work = window * DOC_UNIT * rows * heads * group * HEAD_DIM * 2
    n_long = group * DOC_UNIT if window - each + 1 > MOST_UNITS else 8
    held = (window * DOC_UNIT * 2 * width + 2 * rows * columns * heads) * 2
    return pl.pallas_call(
        functools.partial(attend_kernel, plan),
        out_shape=jax.ShapeDtypeStruct(queries.shape, queries.dtype),
        grid_spec=pltpu.PrefetchScalarGridSpec(
            num_scalar_prefetch=1,
            grid=(),
            in_specs=[anywhere] * (1 + len(pieces) + len(extra)),
            out_specs=anywhere,
            scratch_shapes=[
                pltpu.VMEM((heads, rows, columns), queries.dtype),
                pltpu.VMEM((heads, rows, columns), queries.dtype),
                pltpu.VMEM((window * DOC_UNIT, 2 * width), queries.dtype),
                pltpu.SemaphoreType.DMA((len(slots),)),
                pltpu.SemaphoreType.DMA((heads,)),
                pltpu.SemaphoreType.DMA((heads,)),
                pltpu.VMEM((n_long, 1), jnp.float32),
                pltpu.VMEM((n_long, 2 * HEAD_DIM), jnp.float32),
            ],
        ),
        input_output_aliases={} if before is None else {2 + len(pieces): 0},
        compiler_params=pltpu.CompilerParams(vmem_limit_bytes=held + (12 << 20)),
        cost_estimate=pl.CostEstimate(
            flops=work,
            transcendentals=work // (4 * HEAD_DIM),
            bytes_accessed=2 * rows * columns * heads * 2 + window * DOC_UNIT * width * 4,
        ),
    )(doc_lengths, queries, *[p.array for p in pieces], *extra)


def on_device(queries, keys, values, doc_lengths):
    rows = queries.shape[0]
    heads = keys.shape[1] // HEAD_DIM
    group = queries.shape[1] // keys.shape[1]
    count = lax.axis_size("seq")
    each = rows // DOC_UNIT
    longest = count * each // 2
    window = longest - 1 + each
    units = np.arange(count * each).reshape(count, each)
    if is_cube(count, each):
        low, high = (
            Piece(jnp.concatenate([keys[part], values[part]], axis=1), units[:, u : u + 1])
            for u, part in enumerate((slice(0, DOC_UNIT), slice(DOC_UNIT, rows)))
        )
        pieces = cube_exchange(low, high)
        return in_stages(queries, doc_lengths, *pieces, window, each, group, heads)
    out = None
    parts = PARTS_OF_HEADS
    for part in range(parts):
        first, last = heads * part // parts, heads * (part + 1) // parts
        columns = slice(first * HEAD_DIM, last * HEAD_DIM)
        both = jnp.concatenate([keys[:, columns], values[:, columns]], axis=1)
        pieces = gather_exchange(Piece(both, units))
        out = attend(
            queries, doc_lengths, pieces, window, each, group, first, last - first, out
        )
    return out


def is_cube(count, each):
    return (count, each) == (8, 2)


def solution(mesh):
    rows = P(("grp", "seq"), None)
    return jax.shard_map(on_device, mesh=mesh, in_specs=(rows, rows, rows, P("grp")), out_specs=rows, check_vma=False)
```
